256 devices in a mesh: seq: 32 (over z_hi, x, core), head: 8 (over y, z_lo).
Axes of the slice: x: 4, y: 4, z: 8 (z_hi: 4, z_lo: 2; z = z_hi * 2 + z_lo), core: 2. Of those that a mesh axis runs over, the one named last changes fastest.
Arguments:
- tokens: bfloat16 [4096, 3072], P('seq', 'head'), may hold values from -5 to 5, as said below
- norm_gains: float32 [5, 3072], replicated, may hold values from 0.25 to 1.75
- window: int32 [24], P('head'), may hold values from 16 to 128, as said below
- self_query: bfloat16 [3072, 3072], P(None, 'head')
- self_key_value: bfloat16 [2, 3072, 1024], P(None, None, 'head')
- self_output: bfloat16 [3072, 3072], P('head'), may hold values from -0.4375 to 0.4375
- shared_key_value: bfloat16 [2, 3072, 1024], P(None, None, 'head')
- cross_query: bfloat16 [3, 3072, 3072], P(None, 'seq', 'head')
- cross_output: bfloat16 [3, 3072, 3072], P(None, 'head', 'seq'), may hold values from -0.4375 to 0.4375
- key_blocks: int32 [3, 32, 16], P(None, 'seq'), may hold values from -1 to 31, as said below
Outputs:
- mixed: float32 [4096, 3072], P('seq', 'head')
The draws below stay inside these ranges and needn't reach their ends.
Inputs may be any that keep to these rules, and one draw needn't show every extreme that they name: `tokens`: rows may hold near twins of the rows beside them. Some head has a window of exactly 128 and some head one of exactly 16. `key_blocks`: the row of query block b lists distinct blocks at or before b, the first being b itself; it holds min(16, b + 1) blocks and -1 in the remaining slots.
All inputs are finite; a program needn't handle non-finite values.
Results may differ from the reference program's by a relative error of at most 0.04.
Values may be sent and summed in bfloat16 or wider, within the bound.
A program may use at most 64 MiB of HBM per device.

```python
import math
import jax
import jax.numpy as jnp
from jax import lax

MODEL_WIDTH = 3072
QUERY_HEADS = 24
KEY_VALUE_HEADS = 8
HEAD_WIDTH = 128
KEY_BLOCK_TOKENS = 128
LISTED_BLOCKS = 16
SECTIONS = 3
TOKENS_PER_INDEX = 128
TOKENS = 4096
SEQUENCE_BLOCKS = 32
N_SEQ = 32
N_HEAD = 8


def draw_tokens(key, part):
    drawn = jnp.clip(jax.random.normal(key, (TOKENS, MODEL_WIDTH), jnp.float32), -4.0, 4.0) * 0.5
    return drawn.astype(jnp.bfloat16)


def key_value_offset(key, selected_index):
    unmasked_sample = jax.random.normal(jax.random.fold_in(key, 11 + selected_index), (2, MODEL_WIDTH, KEY_VALUE_HEADS * HEAD_WIDTH), jnp.float32)
    return jnp.clip(unmasked_sample, -6.0, 6.0) / math.sqrt(MODEL_WIDTH)


def query_base(key, selected_index, count):
    unmasked_sample = jax.random.normal(jax.random.fold_in(key, 21 + selected_index), (count, MODEL_WIDTH, QUERY_HEADS * HEAD_WIDTH), jnp.float32)
    noise = jnp.clip(unmasked_sample, -6.0, 6.0) / math.sqrt(MODEL_WIDTH)
    return noise


def draw_self_query(key, part):
    return query_base(key, 0, 1)[0].astype(jnp.bfloat16)


def draw_self_key_value(key, part):
    return key_value_offset(key, 0).astype(jnp.bfloat16)


def draw_shared_key_value(key, part):
    return key_value_offset(key, 1).astype(jnp.bfloat16)


def draw_cross_query(key, part):
    return query_base(key, 1, SECTIONS).astype(jnp.bfloat16)


def draw_window(key, part):
    widths = jax.random.randint(key, (QUERY_HEADS,), TOKENS_PER_INDEX // 8, TOKENS_PER_INDEX + 1, dtype=jnp.int32)
    widest = jax.random.randint(jax.random.fold_in(key, 5), (), 0, QUERY_HEADS, dtype=jnp.int32)
    step_away = jax.random.randint(jax.random.fold_in(key, 6), (), 1, QUERY_HEADS, dtype=jnp.int32)
    narrow = (widest + step_away) % QUERY_HEADS
    heads = jnp.arange(QUERY_HEADS, dtype=jnp.int32)
    widths = jnp.where(heads == widest, TOKENS_PER_INDEX, widths)
    return jnp.where(heads == narrow, TOKENS_PER_INDEX // 8, widths).astype(jnp.int32)


def draw_key_blocks(key, part):
    blocks = jnp.arange(SEQUENCE_BLOCKS, dtype=jnp.int32)
    noise = jax.random.randint(key, (SECTIONS, SEQUENCE_BLOCKS, SEQUENCE_BLOCKS), 0, 1 << 16, dtype=jnp.int32)
    ranked = noise * SEQUENCE_BLOCKS + blocks[None, None, :]
    earlier = blocks[None, None, :] < blocks[None, :, None]
    ranked = jnp.where(earlier, ranked, -1)
    best, picked = jax.lax.top_k(ranked, LISTED_BLOCKS - 1)
    picked = jnp.where(best >= 0, picked.astype(jnp.int32), -1)
    itself = jnp.broadcast_to(blocks[None, :, None], (SECTIONS, SEQUENCE_BLOCKS, 1))
    return jnp.concatenate([itself, picked], axis=2).astype(jnp.int32)


def block_scale(rng, shape, cuts, least, high):
    level = 1.0
    for axis_at, blocks in cuts:
        steps = jax.random.uniform(jax.random.fold_in(jax.random.fold_in(rng, 6), axis_at), (blocks,), jnp.float32, least / len(cuts), high / len(cuts))
        level = level * jnp.repeat(jnp.exp(steps), shape[axis_at] // blocks).reshape((-1,) + (1,) * (len(shape) - 1 - axis_at))
    return level


def centred(rng, dims, width, bound, split=(), kind=jnp.bfloat16):
    entries = jax.random.normal(rng, dims, jnp.float32) * width
    if len(split) > 0:
        entries = block_scale(rng, dims, split, -0.22, 0.18) * entries
    return jnp.clip(entries, min=-bound, max=bound).astype(kind)


def setup_inputs(seed: int = 0) -> dict:
    key_list = jax.random.split(jax.random.key(seed), 11)
    tokens = draw_tokens(jax.random.fold_in(key_list[10], 71), 0)
    norm_gains = jnp.clip(1.0 + 0.15 * jax.random.normal(key_list[1], (SECTIONS + 2, MODEL_WIDTH), jnp.float32), 0.25, 1.75)
    window = draw_window(jax.random.fold_in(key_list[10], 71), 0)
    self_query = draw_self_query(jax.random.fold_in(key_list[10], 71), 0)
    self_key_value = draw_self_key_value(jax.random.fold_in(key_list[10], 71), 0)
    self_output = centred(key_list[5], (QUERY_HEADS * HEAD_WIDTH, MODEL_WIDTH), (QUERY_HEADS * HEAD_WIDTH // 16) ** -0.5, 0.4375, ((0, 8),))
    shared_key_value = draw_shared_key_value(jax.random.fold_in(key_list[10], 71), 0)
    cross_query = draw_cross_query(jax.random.fold_in(key_list[10], 71), 0)
    cross_output = centred(key_list[8], (SECTIONS, QUERY_HEADS * HEAD_WIDTH, MODEL_WIDTH), (QUERY_HEADS * HEAD_WIDTH // 16) ** -0.5, 0.4375, ((1, 8), (2, 32)))
    key_blocks = draw_key_blocks(jax.random.fold_in(key_list[10], 71), 0)
    return {"tokens": tokens, "norm_gains": norm_gains, "window": window, "self_query": self_query, "self_key_value": self_key_value, "self_output": self_output, "shared_key_value": shared_key_value, "cross_query": cross_query, "cross_output": cross_output, "key_blocks": key_blocks}


EPSILON = 1e-06
MASKED = -1e+30

def normed(stream, gain_row):
    values_f = stream.astype(jnp.float32)
    factor = lax.rsqrt(lax.optimization_barrier(jnp.mean(values_f * values_f, axis=1, keepdims=True)) + EPSILON)
    return (values_f * factor * gain_row[None, :]).astype(jnp.bfloat16)

def project(inputs, weight):
    return jnp.dot(inputs, weight, preferred_element_type=jnp.float32).astype(jnp.bfloat16)

def softmax_rows(scores, allowed):
    scores = jnp.where(allowed, scores, MASKED)
    largest = lax.optimization_barrier(jnp.max(scores, axis=-1, keepdims=True))
    weights = jnp.exp(scores - largest)
    return (weights / lax.optimization_barrier(jnp.sum(weights, axis=-1, keepdims=True))).astype(jnp.bfloat16)

def add_branch(stream, context, out_weight):
    group_cols = context.shape[1] // N_HEAD
    total = stream.astype(jnp.float32)
    for part_index in range(N_HEAD):
        piece = context[:, part_index * group_cols:(part_index + 1) * group_cols]
        weight_rows = out_weight[part_index * group_cols:(part_index + 1) * group_cols]
        term = jnp.dot(piece, weight_rows, preferred_element_type=jnp.float32).astype(jnp.bfloat16)
        term = lax.optimization_barrier(term)
        total = total + term.astype(jnp.float32)
    return total

def window_attention(query_matrix, every_key_row, every_value_row, window):
    query_group_width = QUERY_HEADS // KEY_VALUE_HEADS
    key_rows_extended = jnp.concatenate([jnp.zeros((TOKENS_PER_INDEX, KEY_VALUE_HEADS * HEAD_WIDTH), every_key_row.dtype), every_key_row], axis=0)
    value_rows_extended = jnp.concatenate([jnp.zeros((TOKENS_PER_INDEX, KEY_VALUE_HEADS * HEAD_WIDTH), every_value_row.dtype), every_value_row], axis=0)
    window_bounds = window.reshape(KEY_VALUE_HEADS, query_group_width)
    offsets = jnp.arange(TOKENS_PER_INDEX, dtype=jnp.int32)[:, None] + TOKENS_PER_INDEX - jnp.arange(2 * TOKENS_PER_INDEX, dtype=jnp.int32)[None, :]

    def one_block(block):
        window_begin = (block * TOKENS_PER_INDEX).astype(jnp.int32)
        query_portion = lax.dynamic_slice_in_dim(query_matrix, window_begin, TOKENS_PER_INDEX, 0).reshape(TOKENS_PER_INDEX, KEY_VALUE_HEADS, query_group_width, HEAD_WIDTH).astype(jnp.float32)
        key_portion = lax.dynamic_slice_in_dim(key_rows_extended, window_begin, 2 * TOKENS_PER_INDEX, 0).reshape(2 * TOKENS_PER_INDEX, KEY_VALUE_HEADS, HEAD_WIDTH).astype(jnp.float32)
        value_portion = lax.dynamic_slice_in_dim(value_rows_extended, window_begin, 2 * TOKENS_PER_INDEX, 0).reshape(2 * TOKENS_PER_INDEX, KEY_VALUE_HEADS, HEAD_WIDTH).astype(jnp.float32)
        scores = jnp.einsum('tkgd,skd->kgts', query_portion, key_portion) * HEAD_WIDTH ** (-0.5)
        key_pos = window_begin - TOKENS_PER_INDEX + jnp.arange(2 * TOKENS_PER_INDEX, dtype=jnp.int32)
        allowed = (offsets >= 0)[None, None] & (offsets[None, None] < window_bounds[:, :, None, None]) & (key_pos >= 0)[None, None, None, :]
        probs = softmax_rows(scores, allowed)
        context = jnp.einsum('kgts,skd->tkgd', probs.astype(jnp.float32), value_portion)
        return context.reshape(TOKENS_PER_INDEX, QUERY_HEADS * HEAD_WIDTH).astype(jnp.bfloat16)
    return lax.map(one_block, jnp.arange(N_SEQ, dtype=jnp.int32)).reshape(N_SEQ * TOKENS_PER_INDEX, QUERY_HEADS * HEAD_WIDTH)

def listed_attention(query_matrix, cached_key_rows, cached_value_rows, lists):
    query_group_width = QUERY_HEADS // KEY_VALUE_HEADS
    key_lookup_matrix = cached_key_rows.reshape(SEQUENCE_BLOCKS, KEY_BLOCK_TOKENS, KEY_VALUE_HEADS * HEAD_WIDTH)
    value_lookup_matrix = cached_value_rows.reshape(SEQUENCE_BLOCKS, KEY_BLOCK_TOKENS, KEY_VALUE_HEADS * HEAD_WIDTH)
    inner = jnp.arange(KEY_BLOCK_TOKENS, dtype=jnp.int32)

    def one_block(item):
        block, picks = item
        window_begin = (block * KEY_BLOCK_TOKENS).astype(jnp.int32)
        query_portion = lax.dynamic_slice_in_dim(query_matrix, window_begin, KEY_BLOCK_TOKENS, 0).reshape(KEY_BLOCK_TOKENS, KEY_VALUE_HEADS, query_group_width, HEAD_WIDTH).astype(jnp.float32)
        clamped_index = jnp.maximum(picks, 0).astype(jnp.int32)
        key_portion = jnp.take(key_lookup_matrix, clamped_index, axis=0).reshape(LISTED_BLOCKS * KEY_BLOCK_TOKENS, KEY_VALUE_HEADS, HEAD_WIDTH).astype(jnp.float32)
        value_portion = jnp.take(value_lookup_matrix, clamped_index, axis=0).reshape(LISTED_BLOCKS * KEY_BLOCK_TOKENS, KEY_VALUE_HEADS, HEAD_WIDTH).astype(jnp.float32)
        key_pos = (clamped_index[:, None] * KEY_BLOCK_TOKENS + inner[None, :]).reshape(LISTED_BLOCKS * KEY_BLOCK_TOKENS)
        present = jnp.repeat(picks >= 0, KEY_BLOCK_TOKENS)
        allowed = (present[None, :] & (key_pos[None, :] <= (window_begin + inner)[:, None]))[None, None]
        scores = jnp.einsum('tkgd,skd->kgts', query_portion, key_portion) * HEAD_WIDTH ** (-0.5)
        probs = softmax_rows(scores, allowed)
        context = jnp.einsum('kgts,skd->tkgd', probs.astype(jnp.float32), value_portion)
        return context.reshape(KEY_BLOCK_TOKENS, QUERY_HEADS * HEAD_WIDTH).astype(jnp.bfloat16)
    return lax.map(one_block, (jnp.arange(SEQUENCE_BLOCKS, dtype=jnp.int32), lists)).reshape(SEQUENCE_BLOCKS * KEY_BLOCK_TOKENS, QUERY_HEADS * HEAD_WIDTH)

def reference(tokens, norm_gains, window, self_query, self_key_value, self_output, shared_key_value, cross_query, cross_output, key_blocks):
    first = normed(tokens, norm_gains[0])
    query_matrix = project(first, self_query)
    every_key_row = project(first, self_key_value[0])
    every_value_row = project(first, self_key_value[1])
    context = window_attention(query_matrix, every_key_row, every_value_row, window)
    stream = add_branch(tokens, context, self_output)
    cache_in = normed(stream, norm_gains[1])
    cached_key_rows = project(cache_in, shared_key_value[0])
    cached_value_rows = project(cache_in, shared_key_value[1])
    for section in range(SECTIONS):
        section_in = normed(stream, norm_gains[2 + section])
        query_matrix = project(section_in, cross_query[section])
        context = listed_attention(query_matrix, cached_key_rows, cached_value_rows, key_blocks[section])
        stream = add_branch(stream, context, cross_output[section])
    return stream
```

```python
import math

import jax
import jax.numpy as jnp
from jax import lax
from jax.experimental import pallas as pl
from jax.experimental.pallas import tpu as pltpu
from jax.sharding import PartitionSpec as P

MESH = pl.DeviceIdType.MESH
EPSILON = 1e-06
MASKED = -1e30
F32 = jnp.float32
BF16 = jnp.bfloat16
WIDTH = 3072
ROWS = 128
COLS = 384
HEAD = 128
GROUP = 3
PIECE = 96
SCORE_SCALE = HEAD ** (-0.5) * math.log2(math.e)


def rem(a, b):
    return lax.rem(a, jnp.int32(b))


def div(a, b):
    return lax.div(a, jnp.int32(b))


def dot(a, b):
    return jnp.dot(a, b, preferred_element_type=F32)


def dot_t(a, b):
    return lax.dot_general(a, b, (((1,), (1,)), ((), ())), preferred_element_type=F32)


def kernel(
    window_ref,
    blocks_ref,
    tokens_ref,
    gains_ref,
    sq_hbm,
    skv_hbm,
    so_hbm,
    shkv_hbm,
    cq_hbm,
    co_hbm,
    out_ref,
    sq,
    skv,
    so,
    shkv,
    wall,
    xg,
    rs,
    ob,
    xs,
    acc,
    ssq,
    qs,
    ctx,
    halo,
    kc,
    vc,
    sc,
    mx,
    den,
    oacc,
    load_sem,
    own_sem,
    ag_send,
    ag_recv,
    rs_send,
    rs_recv,
    halo_send,
    halo_recv,
    wz_send,
    wz_recv,
    wx_send,
    wx_recv,
    ws_send,
    ws_recv,
    cz_send,
    cz_recv,
    cx_send,
    cx_recv,
    cs_send,
    cs_recv,
):
    seq = lax.axis_index("seq")
    head = lax.axis_index("head")
    core = rem(seq, 2)
    xp = rem(div(seq, 2), 4)
    zh = div(seq, 8)
    yp = div(head, 2)
    zl = rem(head, 2)

    def seq_at(zz, xx, cc):
        return zz * 8 + xx * 2 + cc

    def head_to(k):
        return rem(yp + div(k, 2), 4) * 2 + rem(zl + rem(k, 2), 2)

    def head_from(k):
        return rem(yp + 4 - div(k, 2), 4) * 2 + rem(zl + rem(k, 2), 2)

    z_to = [rem(zh + d, 4) for d in (1, 2, 3)]
    z_from = [rem(zh + 4 - d, 4) for d in (1, 2, 3)]
    x_to = [rem(xp + d, 4) for d in (1, 2, 3)]
    x_from = [rem(xp + 4 - d, 4) for d in (1, 2, 3)]
    sibling = seq_at(zh, xp, 1 - core)
    following = rem(seq + 1, 32)
    previous = rem(seq + 31, 32)

    loads = [
        pltpu.make_async_copy(a, b, load_sem.at[i])
        for i, (a, b) in enumerate(((sq_hbm, sq), (skv_hbm, skv), (so_hbm, so), (shkv_hbm, shkv)))
    ]
    for copy in loads:
        copy.start()

    def piece_source(p):
        return (cq_hbm if p % 2 == 0 else co_hbm).at[p // 2]

    owns = [
        pltpu.make_async_copy(piece_source(p), wall.at[p, zh, xp, core], own_sem.at[p])
        for p in range(6)
    ]
    for copy in owns:
        copy.start()

    barrier = pltpu.get_barrier_semaphore()

    def greet(s, h):
        pl.semaphore_signal(barrier, inc=1, device_id=(s, h), device_id_type=MESH)

    for k in range(1, 8):
        greet(seq, head_to(jnp.int32(k)))
    for zz in z_to:
        greet(seq_at(zz, xp, core), head)
    for xx in x_to:
        greet(seq_at(zh, xx, core), head)
    greet(sibling, head)
    greet(following, head)
    greet(previous, head)
    pl.semaphore_wait(barrier, 16)

    def remote(src, dst, send, recv, s, h):
        return pltpu.make_async_remote_copy(
            src_ref=src, dst_ref=dst, send_sem=send, recv_sem=recv, device_id=(s, h), device_id_type=MESH
        )

    def ag_out(k, src):
        return remote(src, xg.at[head], ag_send.at[k], ag_recv.at[k], seq, head_to(k))

    def ag_in(k):
        return remote(xg.at[head], xg.at[head_from(k)], ag_send.at[k], ag_recv.at[k], seq, head_to(k))

    def ag_start(src):
        def step(k, carry):
            ag_out(k, src).start()
            return carry

        lax.fori_loop(1, 8, step, 0)

    def ag_drain(src):
        def step(k, carry):
            ag_out(k, src).wait_send()
            return carry

        lax.fori_loop(1, 8, step, 0)

    def rs_copy(k):
        return remote(ob.at[k], rs.at[k], rs_send.at[k], rs_recv.at[k], seq, head_to(k))

    def wz_out(p, i):
        return remote(
            piece_source(p), wall.at[p, zh, xp, core], wz_send.at[p, i], wz_recv.at[p, i],
            seq_at(z_to[i], xp, core), head,
        )

    def wz_in(p, i):
        return remote(
            piece_source(p), wall.at[p, z_from[i], xp, core], wz_send.at[p, i], wz_recv.at[p, i],
            seq_at(z_to[i], xp, core), head,
        )

    def wx_out(p, i):
        part = wall.at[p, :, xp, core]
        return remote(part, part, wx_send.at[p, i], wx_recv.at[p, i], seq_at(zh, x_to[i], core), head)

    def wx_in(p, i):
        part = wall.at[p, :, x_from[i], core]
        return remote(part, part, wx_send.at[p, i], wx_recv.at[p, i], seq_at(zh, x_to[i], core), head)

    def ws_out(p):
        part = wall.at[p, :, :, core]
        return remote(part, part, ws_send.at[p], ws_recv.at[p], sibling, head)

    def ws_in(p):
        part = wall.at[p, :, :, 1 - core]
        return remote(part, part, ws_send.at[p], ws_recv.at[p], sibling, head)

    def weight_z(p):
        for i in range(3):
            wz_out(p, i).start()

    def weight_x(p):
        owns[p].wait()
        for i in range(3):
            wz_in(p, i).wait_recv()
        for i in range(3):
            wx_out(p, i).start()

    def weight_s(p):
        for i in range(3):
            wx_in(p, i).wait_recv()
        ws_out(p).start()

    def weight_wait(p):
        ws_in(p).wait_recv()

    cache = (kc, vc)

    def cz_out(c, i):
        part = cache[c].at[zh, xp, core]
        return remote(part, part, cz_send.at[c, i], cz_recv.at[c, i], seq_at(z_to[i], xp, core), head)

    def cz_in(c, i):
        part = cache[c].at[z_from[i], xp, core]
        return remote(part, part, cz_send.at[c, i], cz_recv.at[c, i], seq_at(z_to[i], xp, core), head)

    def cx_out(c, i):
        part = cache[c].at[:, xp, core]
        return remote(part, part, cx_send.at[c, i], cx_recv.at[c, i], seq_at(zh, x_to[i], core), head)

    def cx_in(c, i):
        part = cache[c].at[:, x_from[i], core]
        return remote(part, part, cx_send.at[c, i], cx_recv.at[c, i], seq_at(zh, x_to[i], core), head)

    def cs_out(c):
        part = cache[c].at[:, :, core]
        return remote(part, part, cs_send.at[c], cs_recv.at[c], sibling, head)

    def cs_in(c):
        part = cache[c].at[:, :, 1 - core]
        return remote(part, part, cs_send.at[c], cs_recv.at[c], sibling, head)

    def gain(row, j):
        return gains_ref[row : row + 1, pl.ds(pl.multiple_of(j * COLS, 128), COLS)]

    def rows_of(j):
        return pl.ds(pl.multiple_of(j * COLS, 128), COLS)

    def square_sum(xf):
        sq2 = xf * xf
        return sq2[:, :HEAD] + sq2[:, HEAD : 2 * HEAD] + sq2[:, 2 * HEAD :]

    def row_factor():
        return lax.rsqrt(jnp.sum(ssq[...], axis=1, keepdims=True) / WIDTH + EPSILON)

    def query_block(p, j):
        w = wall[p, div(j, 2), pl.ds(rem(j, 2) * 2, 2)]
        return w.reshape(COLS, COLS)

    def stack_query(factor):
        for g in range(GROUP):
            part = acc[:, g * HEAD : (g + 1) * HEAD]
            qs[g * HEAD : (g + 1) * HEAD, :] = (part * (factor * SCORE_SCALE)).astype(BF16)

    def spread_context():
        inv = 1.0 / jnp.sum(den[...], axis=1, keepdims=True)
        c = (oacc[...] * inv).astype(BF16)
        for g in range(GROUP):
            ctx[:, g * HEAD : (g + 1) * HEAD] = c[g * HEAD : (g + 1) * HEAD, :]

    def reduce_out(block_of):
        def step(k, carry):
            ob[k] = block_of(head_to(k)).astype(BF16)
            rs_copy(k).start()
            return carry

        lax.fori_loop(1, 8, step, 0)
        xs[...] += block_of(head).astype(BF16).astype(F32)

    def reduce_in():
        def step(k, carry):
            rs_copy(k).wait_recv()
            xs[...] += rs[k].astype(F32)
            return carry

        lax.fori_loop(1, 8, step, 0)

    def rs_drain():
        def step(k, carry):
            rs_copy(k).wait_send()
            return carry

        lax.fori_loop(1, 8, step, 0)

    ag_start(tokens_ref)
    weight_z(0)
    xg[head] = tokens_ref[...]
    xs[...] = tokens_ref[...].astype(F32)
    acc[...] = jnp.zeros_like(acc)
    ssq[...] = jnp.zeros_like(ssq)
    loads[0].wait()
    loads[1].wait()

    def first_block(j):
        xf = xg[j].astype(F32)
        ssq[...] += square_sum(xf)
        hb = (xf * gain(0, j)).astype(BF16)
        acc[:, COLS : COLS + HEAD] += dot(hb, skv[0, rows_of(j)])
        acc[:, COLS + HEAD :] += dot(hb, skv[1, rows_of(j)])
        acc[:, :COLS] += dot(hb, sq[rows_of(j)])

    first_block(head)

    def first_step(k, carry):
        ag_in(k).wait_recv()
        first_block(head_from(k))
        return carry

    lax.fori_loop(1, 8, first_step, 0)
    factor = row_factor()
    halo[0] = (acc[:, COLS : COLS + HEAD] * factor).astype(BF16)
    halo[1] = (acc[:, COLS + HEAD :] * factor).astype(BF16)
    halo_copy = remote(halo.at[pl.ds(0, 2)], halo.at[pl.ds(2, 2)], halo_send, halo_recv, following, head)
    halo_copy.start()
    weight_z(1)
    stack_query(factor)
    ag_drain(tokens_ref)
    weight_x(0)

    row = lax.broadcasted_iota(jnp.int32, (ROWS, 1), 0)
    col = lax.broadcasted_iota(jnp.int32, (1, 2 * ROWS), 1)
    offset = row + ROWS - col
    present = (offset >= 0) & (col >= jnp.where(seq == 0, ROWS, 0))
    loads[2].wait()
    halo_copy.wait_recv()
    for g in range(GROUP):
        here = slice(g * HEAD, (g + 1) * HEAD)
        qg = qs[here, :]
        near = jnp.concatenate([dot_t(qg, halo[2]), dot_t(qg, halo[0])], axis=1)
        near = jnp.where(present & (offset < window_ref[g]), near, MASKED)
        top = jnp.max(near, axis=1, keepdims=True)
        weights = jnp.exp2(near - top)
        den[here, :] = weights[:, :ROWS] + weights[:, ROWS:]
        wb = weights.astype(BF16)
        oacc[here, :] = dot(wb[:, :ROWS], halo[3]) + dot(wb[:, ROWS:], halo[1])
    spread_context()
    cvals = ctx[...]
    reduce_out(lambda j: dot(cvals, so[:, pl.ds(pl.multiple_of(j * COLS, 128), COLS)]))
    weight_z(2)
    weight_x(1)
    weight_s(0)
    reduce_in()
    xg[head] = xs[...].astype(BF16)
    own = xg.at[head]
    ag_start(own)
    weight_z(3)
    rs_drain()

    acc[...] = jnp.zeros_like(acc)
    ssq[...] = jnp.zeros_like(ssq)
    loads[3].wait()

    def cache_block(j):
        xf = xg[j].astype(F32)
        ssq[...] += square_sum(xf)
        hb = (xf * gain(1, j)).astype(BF16)
        acc[:, COLS : COLS + HEAD] += dot(hb, shkv[0, rows_of(j)])
        acc[:, COLS + HEAD :] += dot(hb, shkv[1, rows_of(j)])

    cache_block(head)

    def cache_step(k, carry):
        ag_in(k).wait_recv()
        cache_block(head_from(k))
        return carry

    lax.fori_loop(1, 8, cache_step, 0)
    factor = row_factor()
    kc[zh, xp, core] = (acc[:, COLS : COLS + HEAD] * factor).astype(BF16)
    for i in range(3):
        cz_out(0, i).start()
    vc[zh, xp, core] = (acc[:, COLS + HEAD :] * factor).astype(BF16)
    for i in range(3):
        cz_out(1, i).start()
    weight_s(1)
    weight_wait(0)

    def query0_step(j, carry):
        hb = (xg[j].astype(F32) * gain(2, j)).astype(BF16)
        acc[:, :COLS] += dot(hb, query_block(0, j))
        return carry

    lax.fori_loop(0, 8, query0_step, 0)
    stack_query(factor)
    for c in range(2):
        for i in range(3):
            cz_in(c, i).wait_recv()
        for i in range(3):
            cx_out(c, i).start()
    weight_x(2)
    weight_z(4)
    for c in range(2):
        for i in range(3):
            cx_in(c, i).wait_recv()
        cs_out(c).start()
    ag_drain(own)

    tall_row = rem(lax.broadcasted_iota(jnp.int32, (GROUP * ROWS, 1), 0), ROWS)
    causal_col = jnp.where(col < ROWS, col, -1)

    for section in range(3):
        if section > 0:
            ag_start(own)
            rs_drain()
            if section == 1:
                weight_z(5)
                weight_x(4)
                weight_s(3)
            else:
                weight_s(5)
            acc[...] = jnp.zeros_like(acc)
            ssq[...] = jnp.zeros_like(ssq)
            weight_wait(2 * section)

            def query_block_step(j, section=section):
                xf = xg[j].astype(F32)
                ssq[...] += square_sum(xf)
                hb = (xf * gain(2 + section, j)).astype(BF16)
                acc[:, :COLS] += dot(hb, query_block(2 * section, j))

            query_block_step(head)

            def query_step(k, carry, query_block_step=query_block_step):
                ag_in(k).wait_recv()
                query_block_step(head_from(k))
                return carry

            lax.fori_loop(1, 8, query_step, 0)
            stack_query(row_factor())
            ag_drain(own)

        if section == 0:
            cs_in(0).wait_recv()
        qv = qs[...]
        mx[...] = jnp.full_like(mx, MASKED)

        def pick(ref, i):
            n = jnp.maximum(blocks_ref[section, 0, i], 0)
            return ref[div(n, 8), rem(div(n, 2), 4), rem(n, 2)]

        def score_step(i, carry, qv=qv, pick=pick, section=section):
            keys = jnp.concatenate([pick(kc, 2 * i), pick(kc, 2 * i + 1)], axis=0)
            t = dot_t(qv, keys)
            low = jnp.where(blocks_ref[section, 0, 2 * i] >= 0, 0.0, MASKED)
            high = jnp.where(blocks_ref[section, 0, 2 * i + 1] >= 0, 0.0, MASKED)
            bias = jnp.where(col < ROWS, low, high)
            t = jnp.where(causal_col <= tall_row + jnp.where(i == 0, 0, 4096), t, MASKED) + bias
            sc[i] = t
            mx[...] = jnp.maximum(mx[...], jnp.maximum(t[:, :HEAD], t[:, HEAD:]))
            return carry

        lax.fori_loop(0, 8, score_step, 0)
        top = jnp.max(mx[...], axis=1, keepdims=True)
        den[...] = jnp.zeros_like(den)
        oacc[...] = jnp.zeros_like(oacc)
        if section == 0:
            cs_in(1).wait_recv()

        def value_step(i, carry, top=top, pick=pick):
            weights = jnp.exp2(sc[i] - top)
            den[...] += weights[:, :HEAD] + weights[:, HEAD:]
            values = jnp.concatenate([pick(vc, 2 * i), pick(vc, 2 * i + 1)], axis=0)
            oacc[...] += dot(weights.astype(BF16), values)
            return carry

        lax.fori_loop(0, 8, value_step, 0)
        spread_context()
        weight_wait(2 * section + 1)
        cvals = ctx[...]
        reduce_out(lambda j, cvals=cvals, section=section: dot_t(cvals, query_block(2 * section + 1, j)))
        if section == 0:
            weight_x(3)
            weight_s(2)
        elif section == 1:
            weight_x(5)
            weight_s(4)
        reduce_in()
        if section < 2:
            xg[head] = xs[...].astype(BF16)
    out_ref[...] = xs[...]

    rs_drain()
    halo_copy.wait_send()
    for p in range(6):
        for i in range(3):
            wz_out(p, i).wait_send()
            wx_out(p, i).wait_send()
        ws_out(p).wait_send()
    for c in range(2):
        for i in range(3):
            cz_out(c, i).wait_send()
            cx_out(c, i).wait_send()
        cs_out(c).wait_send()


def body(
    tokens,
    norm_gains,
    window,
    self_query,
    self_key_value,
    self_output,
    shared_key_value,
    cross_query,
    cross_output,
    key_blocks,
):
    vmem = pl.BlockSpec(memory_space=pltpu.VMEM)
    smem = pl.BlockSpec(memory_space=pltpu.SMEM)
    hbm = pl.BlockSpec(memory_space=pl.ANY)
    dma = pltpu.SemaphoreType.DMA
    return pl.pallas_call(
        kernel,
        out_shape=jax.ShapeDtypeStruct((ROWS, COLS), F32),
        in_specs=[smem, smem, vmem, vmem] + [hbm] * 6,
        out_specs=vmem,
        scratch_shapes=[
            pltpu.VMEM((WIDTH, COLS), BF16),
            pltpu.VMEM((2, WIDTH, HEAD), BF16),
            pltpu.VMEM((COLS, WIDTH), BF16),
            pltpu.VMEM((2, WIDTH, HEAD), BF16),
            pltpu.VMEM((6, 4, 4, 2, PIECE, COLS), BF16),
            pltpu.VMEM((8, ROWS, COLS), BF16),
            pltpu.VMEM((8, ROWS, COLS), BF16),
            pltpu.VMEM((8, ROWS, COLS), BF16),
            pltpu.VMEM((ROWS, COLS), F32),
            pltpu.VMEM((ROWS, COLS + 2 * HEAD), F32),
            pltpu.VMEM((ROWS, HEAD), F32),
            pltpu.VMEM((GROUP * ROWS, HEAD), BF16),
            pltpu.VMEM((ROWS, COLS), BF16),
            pltpu.VMEM((4, ROWS, HEAD), BF16),
            pltpu.VMEM((4, 4, 2, ROWS, HEAD), BF16),
            pltpu.VMEM((4, 4, 2, ROWS, HEAD), BF16),
            pltpu.VMEM((8, GROUP * ROWS, 2 * HEAD), F32),
            pltpu.VMEM((GROUP * ROWS, HEAD), F32),
            pltpu.VMEM((GROUP * ROWS, HEAD), F32),
            pltpu.VMEM((GROUP * ROWS, HEAD), F32),
            dma((4,)),
            dma((6,)),
            dma((8,)),
            dma((8,)),
            dma((8,)),
            dma((8,)),
            dma,
            dma,
            dma((6, 3)),
            dma((6, 3)),
            dma((6, 3)),
            dma((6, 3)),
            dma((6,)),
            dma((6,)),
            dma((2, 3)),
            dma((2, 3)),
            dma((2, 3)),
            dma((2, 3)),
            dma((2,)),
            dma((2,)),
        ],
        compiler_params=pltpu.CompilerParams(
            collective_id=0, has_side_effects=True, vmem_limit_bytes=60 * 1024 * 1024
        ),
        name="window",
    )(
        window,
        key_blocks,
        tokens,
        norm_gains,
        self_query,
        self_key_value,
        self_output,
        shared_key_value,
        cross_query,
        jnp.swapaxes(cross_output, 1, 2),
    )


def solution(mesh):
    placed = (
        P("seq", "head"),
        P(),
        P("head"),
        P(None, "head"),
        P(None, None, "head"),
        P("head", None),
        P(None, None, "head"),
        P(None, "seq", "head"),
        P(None, "head", "seq"),
        P(None, "seq", None),
    )
    return jax.shard_map(
        body, mesh=mesh, in_specs=placed, out_specs=P("seq", "head"), check_vma=False
    )
```

```python
import math

import jax
import jax.numpy as jnp
from jax import lax
from jax.experimental import pallas as pl
from jax.experimental.pallas import tpu as pltpu
from jax.sharding import PartitionSpec as P

MESH = pl.DeviceIdType.MESH
EPSILON = 1e-06
MASKED = -1e30
F32 = jnp.float32
BF16 = jnp.bfloat16
WIDTH = 3072
ROWS = 128
COLS = 384
HEAD = 128
GROUP = 3
PIECE = 96
HALF = 64
SCORE_SCALE = HEAD ** (-0.5) * math.log2(math.e)


mark = jax.named_scope


def rem(a, b):
    return lax.rem(a, jnp.int32(b))


def div(a, b):
    return lax.div(a, jnp.int32(b))


def dot(a, b):
    return jnp.dot(a, b, preferred_element_type=F32)


def dot_t(a, b):
    return lax.dot_general(a, b, (((1,), (1,)), ((), ())), preferred_element_type=F32)


def kernel(
    window_ref,
    blocks_ref,
    tokens_hbm,
    gains_hbm,
    sq_hbm,
    skv_hbm,
    so_hbm,
    shkv_hbm,
    cq_hbm,
    co_hbm,
    out_ref,
    gains_ref,
    sq,
    skv,
    so,
    shkv,
    wall,
    xg,
    rs,
    ob,
    xs,
    acc,
    qs,
    ctx,
    own_kv,
    halo,
    kc,
    vc,
    sc,
    den,
    oacc,
    load_sem,
    own_sem,
    ag_send,
    ag_recv,
    rs_send,
    rs_recv,
    halo_send,
    halo_recv,
    wz_send,
    wz_recv,
    wx_send,
    wx_recv,
    wy_send,
    wy_recv,
    ws_send,
    ws_recv,
    cz_send,
    cz_recv,
    cx_send,
    cx_recv,
    cs_send,
    cs_recv,
):
    seq = lax.axis_index("seq")
    head = lax.axis_index("head")
    core = rem(seq, 2)
    xp = rem(div(seq, 2), 4)
    zh = div(seq, 8)
    yp = div(head, 2)
    zl = rem(head, 2)

    def seq_at(zz, xx, cc):
        return zz * 8 + xx * 2 + cc

    def head_to(k):
        return rem(yp + div(k, 2), 4) * 2 + rem(zl + rem(k, 2), 2)

    def head_from(k):
        return rem(yp + 4 - div(k, 2), 4) * 2 + rem(zl + rem(k, 2), 2)

    z_to = [rem(zh + d, 4) for d in (1, 2, 3)]
    z_from = [rem(zh + 4 - d, 4) for d in (1, 2, 3)]
    x_to = [rem(xp + d, 4) for d in (1, 2, 3)]
    x_from = [rem(xp + 4 - d, 4) for d in (1, 2, 3)]
    sibling = seq_at(zh, xp, 1 - core)
    following = rem(seq + 1, 32)
    previous = rem(seq + 31, 32)

    def rows_half(h):
        return pl.ds(h * HALF, HALF)

    barrier = pltpu.get_barrier_semaphore()

    def greet(s, h):
        pl.semaphore_signal(barrier, inc=1, device_id=(s, h), device_id_type=MESH)

    for zz in z_to:
        greet(seq_at(zz, xp, core), head)
    for k in range(1, 8):
        greet(seq, head_to(jnp.int32(k)))
    for xx in x_to:
        greet(seq_at(zh, xx, core), head)
    greet(sibling, head)
    greet(following, head)
    greet(previous, head)

    loads = [
        pltpu.make_async_copy(a, b, load_sem.at[i])
        for i, (a, b) in enumerate(
            (
                (tokens_hbm.at[rows_half(0)], xg.at[0, head]),
                (tokens_hbm.at[rows_half(1)], xg.at[1, head]),
                (gains_hbm, gains_ref),
                (skv_hbm, skv),
                (sq_hbm, sq),
                (so_hbm, so),
                (shkv_hbm, shkv),
            )
        )
    ]
    for copy in loads:
        copy.start()

    def piece_source(p):
        return (cq_hbm if p % 2 == 0 else co_hbm).at[p // 2]

    owns = [
        pltpu.make_async_copy(piece_source(p), wall.at[p, zh, xp, core], own_sem.at[p])
        for p in range(6)
    ]
    for copy in owns:
        copy.start()

    with mark("barrier"):
        pl.semaphore_wait(barrier, 16)

    def remote(src, dst, send, recv, s, h):
        return pltpu.make_async_remote_copy(
            src_ref=src, dst_ref=dst, send_sem=send, recv_sem=recv, device_id=(s, h), device_id_type=MESH
        )

    beside_z = yp * 2 + 1 - zl

    def ag_out(h, k, src):
        return remote(src, xg.at[h, head], ag_send.at[h, k], ag_recv.at[h, k], seq, head_to(jnp.int32(k)))

    def ag_pass(h, k):
        part = xg.at[h, beside_z]
        return remote(part, part, ag_send.at[h, k], ag_recv.at[h, k], seq, head_to(jnp.int32(k - 1)))

    def ag_in(h, k):
        return remote(
            xg.at[h, head], xg.at[h, head_from(jnp.int32(k))], ag_send.at[h, k], ag_recv.at[h, k], seq,
            head_to(jnp.int32(k)),
        )

    def ag_start(h, src):
        for k in (1, 2, 6, 4):
            ag_out(h, k, src).start()

    def ag_forward(h):
        with mark("forward"):
            ag_in(h, 1).wait_recv()
            for k in (3, 7, 5):
                ag_pass(h, k).start()

    def ag_near(h):
        for k in (2, 6, 4):
            ag_in(h, k).wait_recv()

    def ag_far(h):
        for k in (3, 7, 5):
            ag_in(h, k).wait_recv()

    def ag_drain(h, src):
        for k in (1, 2, 6, 4):
            ag_out(h, k, src).wait_send()
        for k in (3, 7, 5):
            ag_pass(h, k).wait_send()

    def rs_copy(h, k):
        to = head_to(jnp.int32(k))
        return remote(ob.at[h, to], rs.at[h, k], rs_send.at[h, k], rs_recv.at[h, k], seq, to)

    def wz_out(p, i):
        return remote(
            piece_source(p), wall.at[p, zh, xp, core], wz_send.at[p, i], wz_recv.at[p, i],
            seq_at(z_to[i], xp, core), head,
        )

    def wz_in(p, i):
        return remote(
            piece_source(p), wall.at[p, z_from[i], xp, core], wz_send.at[p, i], wz_recv.at[p, i],
            seq_at(z_to[i], xp, core), head,
        )

    beside = (x_to[0], x_to[2])

    def wx_out(p, i):
        part = wall.at[p, :, xp, core]
        return remote(part, part, wx_send.at[p, i], wx_recv.at[p, i], seq_at(zh, beside[i], core), head)

    def wx_in(p, i):
        part = wall.at[p, :, beside[1 - i], core]
        return remote(part, part, wx_send.at[p, i], wx_recv.at[p, i], seq_at(zh, beside[i], core), head)

    def wy_out(p, i):
        part = wall.at[p, pl.ds(2 * i, 2), beside[1 - i], core]
        return remote(part, part, wy_send.at[p, i], wy_recv.at[p, i], seq_at(zh, beside[i], core), head)

    def wy_in(p, i):
        part = wall.at[p, pl.ds(2 * i, 2), x_to[1], core]
        return remote(part, part, wy_send.at[p, i], wy_recv.at[p, i], seq_at(zh, beside[i], core), head)

    def ws_out(p):
        part = wall.at[p, :, :, core]
        return remote(part, part, ws_send.at[p], ws_recv.at[p], sibling, head)

    def ws_in(p):
        part = wall.at[p, :, :, 1 - core]
        return remote(part, part, ws_send.at[p], ws_recv.at[p], sibling, head)

    def weight_z(p):
        for i in range(3):
            wz_out(p, i).start()

    def weight_x(p):
        with mark("weight_x"):
            owns[p].wait()
            for i in range(3):
                wz_in(p, i).wait_recv()
            for i in range(2):
                wx_out(p, i).start()

    def weight_y(p):
        with mark("weight_y"):
            for i in range(2):
                wx_in(p, i).wait_recv()
                wy_out(p, i).start()

    def weight_s(p):
        with mark("weight_s"):
            for i in range(2):
                wy_in(p, i).wait_recv()
            ws_out(p).start()

    def weight_wait(p):
        with mark("weight_wait"):
            ws_in(p).wait_recv()

    cache = (kc, vc)

    def cz_part(c, h, zz):
        return cache[c].at[zz, xp, core, rows_half(h)]

    def cz_out(c, h, i):
        part = cz_part(c, h, zh)
        return remote(part, part, cz_send.at[c, h, i], cz_recv.at[c, h, i], seq_at(z_to[i], xp, core), head)

    def cz_in(c, h, i):
        part = cz_part(c, h, z_from[i])
        return remote(part, part, cz_send.at[c, h, i], cz_recv.at[c, h, i], seq_at(z_to[i], xp, core), head)

    def cx_out(c, h, m, i):
        part = cz_part(c, h, rem(zh + 4 - m, 4))
        return remote(part, part, cx_send.at[c, h, m, i], cx_recv.at[c, h, m, i], seq_at(zh, x_to[i], core), head)

    def cx_in(c, h, m, i):
        part = cache[c].at[rem(zh + 4 - m, 4), x_from[i], core, rows_half(h)]
        return remote(part, part, cx_send.at[c, h, m, i], cx_recv.at[c, h, m, i], seq_at(zh, x_to[i], core), head)

    def cs_out(c, h):
        part = cache[c].at[:, :, core, rows_half(h)]
        return remote(part, part, cs_send.at[c, h], cs_recv.at[c, h], sibling, head)

    def cs_in(c, h):
        part = cache[c].at[:, :, 1 - core, rows_half(h)]
        return remote(part, part, cs_send.at[c, h], cs_recv.at[c, h], sibling, head)

    def cols_of(j):
        return pl.ds(pl.multiple_of(j * COLS, 128), COLS)

    def gain(row, j):
        return gains_ref[row : row + 1, cols_of(j)]

    def square_sum(xf):
        sq2 = xf * xf
        return sq2[:, :HEAD] + sq2[:, HEAD : 2 * HEAD] + sq2[:, 2 * HEAD :]

    def row_factor(squares):
        return lax.rsqrt(jnp.sum(squares, axis=1, keepdims=True) / WIDTH + EPSILON)

    def plane(h, zz, row):
        parts, squares = [], 0.0
        for y in range(4):
            j = y * 2 + zz
            xf = xg[h, j].astype(F32)
            squares = squares + square_sum(xf)
            parts.append((xf * gain(row, j)).astype(BF16))
        return jnp.concatenate(parts, axis=1), squares

    def key_value_rows(ref, zz):
        keys = jnp.concatenate([ref[0, cols_of(y * 2 + zz)] for y in range(4)], axis=0)
        values = jnp.concatenate([ref[1, cols_of(y * 2 + zz)] for y in range(4)], axis=0)
        return jnp.concatenate([keys, values], axis=1)

    def piece_rows(p, zz):
        return wall[p, :, pl.ds(zz * 2, 2)].reshape(4 * COLS, COLS)

    def stack_query(h, full, factor):
        scaled = full * (factor * SCORE_SCALE)
        for g in range(GROUP):
            qs[h, g * HALF : (g + 1) * HALF, :] = scaled[:, g * HEAD : (g + 1) * HEAD].astype(BF16)

    def spread_context():
        inv = 1.0 / jnp.sum(den[...], axis=1, keepdims=True)
        c = (oacc[...] * inv).astype(BF16)
        for g in range(GROUP):
            ctx[:, g * HEAD : (g + 1) * HEAD] = c[g * HALF : (g + 1) * HALF, :]

    far = (3, 7, 5, 1)
    near = (4, 2, 6)

    def reduce_out(h, plane_of):
        with mark("rs_out"):
            for zz, ks in ((1 - zl, far), (zl, near)):
                for y, block in enumerate(plane_of(zz)):
                    ob[h, y * 2 + zz] = block.astype(BF16)
                for k in ks:
                    rs_copy(h, k).start()

    def reduce_in(h):
        with mark("rs_in"):
            for k in near + far:
                rs_copy(h, k).wait_recv()
            total = xs[h] + ob[h, head].astype(F32)
            for k in near + far:
                total = total + rs[h, k].astype(F32)
        return total

    def rs_drain(h):
        for k in near + far:
            rs_copy(h, k).wait_send()

    def own_part(h):
        return xg.at[h, head]

    for h in range(2):
        ag_start(h, tokens_hbm.at[rows_half(h)])
    weight_z(0)
    for h in range(2):
        ag_forward(h)
    weight_z(1)
    for copy in loads[:5]:
        copy.wait()

    def halo_of(h):
        return remote(
            own_kv.at[:, rows_half(h)], halo.at[:, rows_half(h)], halo_send.at[h], halo_recv.at[h], following, head
        )

    for h in range(2):
        xs[h] = xg[h, head].astype(F32)
        with mark("ag0"):
            ag_near(h)
            hb, squares = plane(h, zl, 0)
            acc[:, COLS:] = dot(hb, key_value_rows(skv, zl))
            acc[:, :COLS] = dot(hb, jnp.concatenate([sq[cols_of(y * 2 + zl)] for y in range(4)], axis=0))
            ag_far(h)
            hb, more = plane(h, 1 - zl, 0)
            factor = row_factor(squares + more)
            kv = (acc[:, COLS:] + dot(hb, key_value_rows(skv, 1 - zl))) * factor
            own_kv[0, rows_half(h)] = kv[:, :HEAD].astype(BF16)
            own_kv[1, rows_half(h)] = kv[:, HEAD:].astype(BF16)
            halo_of(h).start()
            full = acc[:, :COLS] + dot(
                hb, jnp.concatenate([sq[cols_of(y * 2 + 1 - zl)] for y in range(4)], axis=0)
            )
            stack_query(h, full, factor)

    weight_z(2)
    for h in range(2):
        ag_drain(h, tokens_hbm.at[rows_half(h)])

    col = lax.broadcasted_iota(jnp.int32, (1, 2 * ROWS), 1)
    loads[5].wait()
    with mark("halo"):
        for h in range(2):
            halo_of(h).wait_recv()
    weight_x(0)
    for h in range(2):
        row = lax.broadcasted_iota(jnp.int32, (HALF, 1), 0) + h * HALF
        offset = row + ROWS - col
        present = (offset >= 0) & (col >= jnp.where(seq == 0, ROWS, 0))
        with mark("self_attn"):
            for g in range(GROUP):
                here = slice(g * HALF, (g + 1) * HALF)
                qg = qs[h, here, :]
                score = jnp.concatenate([dot_t(qg, halo[0]), dot_t(qg, own_kv[0])], axis=1)
                score = jnp.where(present & (offset < window_ref[g]), score, MASKED)
                top = jnp.max(score, axis=1, keepdims=True)
                weights = jnp.exp2(score - top)
                den[here, :] = weights[:, :ROWS] + weights[:, ROWS:]
                wb = weights.astype(BF16)
                oacc[here, :] = dot(wb[:, :ROWS], halo[1]) + dot(wb[:, ROWS:], own_kv[1])
            spread_context()
        cvals = ctx[...]
        reduce_out(h, lambda zz, cvals=cvals: [dot(cvals, so[:, cols_of(y * 2 + zz)]) for y in range(4)])
    weight_y(0)
    weight_x(1)
    for h in range(2):
        total = reduce_in(h)
        xs[h] = total
        xg[h, head] = total.astype(BF16)
        ag_start(h, own_part(h))
        if h == 0:
            ag_forward(0)
        else:
            weight_z(3)
            weight_s(0)
    loads[6].wait()

    factors = []
    for h in range(2):
        with mark("ag1"):
            ag_near(h)
            hb, squares = plane(h, zl, 1)
            acc[:, COLS:] = dot(hb, key_value_rows(shkv, zl))
            if h == 0:
                ag_forward(1)
                weight_y(1)
                weight_x(2)
            ag_far(h)
            hb, more = plane(h, 1 - zl, 1)
            factor = row_factor(squares + more)
            kv = (acc[:, COLS:] + dot(hb, key_value_rows(shkv, 1 - zl))) * factor
        factors.append(factor)
        for c in range(2):
            cache[c][zh, xp, core, rows_half(h)] = kv[:, c * HEAD : (c + 1) * HEAD].astype(BF16)
            for i in range(3):
                cz_out(c, h, i).start()
            for i in range(3):
                cx_out(c, h, 0, i).start()
    weight_s(1)
    weight_wait(0)
    for h in range(2):
        rs_drain(h)
        with mark("q0"):
            full = 0.0
            for zz in (0, 1):
                hb, _ = plane(h, zz, 2)
                full = full + dot(hb, piece_rows(0, zz))
        stack_query(h, full, factors[h])
        ag_drain(h, own_part(h))
    with mark("cache_z"):
        for h in range(2):
            for c in range(2):
                for m in (1, 2, 3):
                    cz_in(c, h, m - 1).wait_recv()
                    for i in range(3):
                        cx_out(c, h, m, i).start()
    weight_y(2)
    weight_x(3)
    weight_z(4)
    with mark("cache_x"):
        for h in range(2):
            for c in range(2):
                for m in range(4):
                    for i in range(3):
                        cx_in(c, h, m, i).wait_recv()
                cs_out(c, h).start()
    weight_s(2)
    with mark("cache_s"):
        for h in range(2):
            for c in range(2):
                cs_in(c, h).wait_recv()

    half_row = rem(lax.broadcasted_iota(jnp.int32, (GROUP * HALF, 1), 0), HALF)
    causal_col = jnp.where(col < ROWS, col, -1)

    for section in range(3):
        for h in range(2):
            if section > 0:
                if h == 0:
                    weight_wait(2 * section)
                with mark("ag"):
                    ag_near(h)
                    hb, squares = plane(h, zl, 2 + section)
                    acc[:, :COLS] = dot(hb, piece_rows(2 * section, zl))
                    ag_far(h)
                    hb, more = plane(h, 1 - zl, 2 + section)
                    full = acc[:, :COLS] + dot(hb, piece_rows(2 * section, 1 - zl))
                    stack_query(h, full, row_factor(squares + more))

            qv = qs[h]

            def pick(ref, i, section=section):
                n = jnp.maximum(blocks_ref[section, 0, i], 0)
                return ref[div(n, 8), rem(div(n, 2), 4), rem(n, 2)]

            with mark("score"):
                best = None
                for i in range(8):
                    keys = jnp.concatenate([pick(kc, 2 * i), pick(kc, 2 * i + 1)], axis=0)
                    t = dot_t(qv, keys)
                    low = jnp.where(blocks_ref[section, 0, 2 * i] >= 0, 0.0, MASKED)
                    high = jnp.where(blocks_ref[section, 0, 2 * i + 1] >= 0, 0.0, MASKED)
                    if i == 0:
                        t = jnp.where(causal_col <= half_row + h * HALF, t, MASKED)
                    t = t + jnp.where(col < ROWS, low, high)
                    sc[i] = t
                    pair = jnp.maximum(t[:, :HEAD], t[:, HEAD:])
                    best = pair if best is None else jnp.maximum(best, pair)
                top = jnp.max(best, axis=1, keepdims=True)
            if section > 0:
                if h == 0:
                    ag_forward(1)
                ag_drain(h, own_part(h))

            with mark("value"):
                dens, outs = None, None
                for i in range(8):
                    weights = jnp.exp2(sc[i] - top)
                    part = weights[:, :HEAD] + weights[:, HEAD:]
                    dens = part if dens is None else dens + part
                    values = jnp.concatenate([pick(vc, 2 * i), pick(vc, 2 * i + 1)], axis=0)
                    part = dot(weights.astype(BF16), values)
                    outs = part if outs is None else outs + part
                den[...] = dens
                oacc[...] = outs
            spread_context()
            if h == 0:
                weight_wait(2 * section + 1)
            cvals = ctx[...]
            if section > 0:
                rs_drain(h)

            def plane_of(zz, cvals=cvals, section=section):
                wide = dot_t(cvals, piece_rows(2 * section + 1, zz))
                return [wide[:, y * COLS : (y + 1) * COLS] for y in range(4)]

            reduce_out(h, plane_of)
            if section == 0 and h == 0:
                weight_y(3)
                weight_x(4)
                weight_z(5)
            elif section == 1 and h == 0:
                weight_s(4)
            elif section == 1 and h == 1:
                weight_y(5)
        for h in range(2):
            total = reduce_in(h)
            if section < 2:
                xs[h] = total
                xg[h, head] = total.astype(BF16)
                ag_start(h, own_part(h))
                if h == 0:
                    ag_forward(0)
            else:
                out_ref[rows_half(h), :] = total
            if section == 0 and h == 0:
                weight_s(3)
            elif section == 0 and h == 1:
                weight_y(4)
                weight_x(5)
            elif section == 1 and h == 1:
                weight_s(5)
    for h in range(2):
        rs_drain(h)

    for h in range(2):
        halo_of(h).wait_send()
    for p in range(6):
        for i in range(3):
            wz_out(p, i).wait_send()
        for i in range(2):
            wx_out(p, i).wait_send()
            wy_out(p, i).wait_send()
        ws_out(p).wait_send()
    for c in range(2):
        for h in range(2):
            for i in range(3):
                cz_out(c, h, i).wait_send()
                for m in range(4):
                    cx_out(c, h, m, i).wait_send()
            cs_out(c, h).wait_send()


def body(
    tokens,
    norm_gains,
    window,
    self_query,
    self_key_value,
    self_output,
    shared_key_value,
    cross_query,
    cross_output,
    key_blocks,
):
    vmem = pl.BlockSpec(memory_space=pltpu.VMEM)
    smem = pl.BlockSpec(memory_space=pltpu.SMEM)
    hbm = pl.BlockSpec(memory_space=pl.ANY)
    dma = pltpu.SemaphoreType.DMA
    return pl.pallas_call(
        kernel,
        out_shape=jax.ShapeDtypeStruct((ROWS, COLS), F32),
        in_specs=[smem, smem] + [hbm] * 8,
        out_specs=vmem,
        scratch_shapes=[
            pltpu.VMEM((5, WIDTH), F32),
            pltpu.VMEM((WIDTH, COLS), BF16),
            pltpu.VMEM((2, WIDTH, HEAD), BF16),
            pltpu.VMEM((COLS, WIDTH), BF16),
            pltpu.VMEM((2, WIDTH, HEAD), BF16),
            pltpu.VMEM((6, 4, 4, 2, PIECE, COLS), BF16),
            pltpu.VMEM((2, 8, HALF, COLS), BF16),
            pltpu.VMEM((2, 8, HALF, COLS), BF16),
            pltpu.VMEM((2, 8, HALF, COLS), BF16),
            pltpu.VMEM((2, HALF, COLS), F32),
            pltpu.VMEM((HALF, COLS + 2 * HEAD), F32),
            pltpu.VMEM((2, GROUP * HALF, HEAD), BF16),
            pltpu.VMEM((HALF, COLS), BF16),
            pltpu.VMEM((2, ROWS, HEAD), BF16),
            pltpu.VMEM((2, ROWS, HEAD), BF16),
            pltpu.VMEM((4, 4, 2, ROWS, HEAD), BF16),
            pltpu.VMEM((4, 4, 2, ROWS, HEAD), BF16),
            pltpu.VMEM((8, GROUP * HALF, 2 * HEAD), F32),
            pltpu.VMEM((GROUP * HALF, HEAD), F32),
            pltpu.VMEM((GROUP * HALF, HEAD), F32),
            dma((7,)),
            dma((6,)),
            dma((2, 8)),
            dma((2, 8)),
            dma((2, 8)),
            dma((2, 8)),
            dma((2,)),
            dma((2,)),
            dma((6, 3)),
            dma((6, 3)),
            dma((6, 2)),
            dma((6, 2)),
            dma((6, 2)),
            dma((6, 2)),
            dma((6,)),
            dma((6,)),
            dma((2, 2, 3)),
            dma((2, 2, 3)),
            dma((2, 2, 4, 3)),
            dma((2, 2, 4, 3)),
            dma((2, 2)),
            dma((2, 2)),
        ],
        compiler_params=pltpu.CompilerParams(
            collective_id=0, has_side_effects=True, vmem_limit_bytes=60 * 1024 * 1024
        ),
        name="window",
    )(
        window,
        key_blocks,
        tokens,
        norm_gains,
        self_query,
        self_key_value,
        self_output,
        shared_key_value,
        cross_query,
        jnp.swapaxes(cross_output, 1, 2),
    )


def solution(mesh):
    placed = (
        P("seq", "head"),
        P(),
        P("head"),
        P(None, "head"),
        P(None, None, "head"),
        P("head", None),
        P(None, None, "head"),
        P(None, "seq", "head"),
        P(None, "head", "seq"),
        P(None, "seq", None),
    )
    return jax.shard_map(
        body, mesh=mesh, in_specs=placed, out_specs=P("seq", "head"), check_vma=False
    )
```

```python
import math

import jax
import jax.numpy as jnp
from jax import lax
from jax.experimental import pallas as pl
from jax.experimental.pallas import tpu as pltpu
from jax.sharding import PartitionSpec as P

MESH = pl.DeviceIdType.MESH
EPSILON = 1e-06
MASKED = -1e30
F32 = jnp.float32
BF16 = jnp.bfloat16
WIDTH = 3072
ROWS = 128
COLS = 384
HEAD = 128
GROUP = 3
PIECE = 96
HALF = 64
SCORE_SCALE = HEAD ** (-0.5) * math.log2(math.e)


mark = jax.named_scope


def rem(a, b):
    return lax.rem(a, jnp.int32(b))


def div(a, b):
    return lax.div(a, jnp.int32(b))


def dot(a, b):
    return jnp.dot(a, b, preferred_element_type=F32)


def dot_t(a, b):
    return lax.dot_general(a, b, (((1,), (1,)), ((), ())), preferred_element_type=F32)


def kernel(
    window_ref,
    blocks_ref,
    tokens_hbm,
    gains_hbm,
    sq_hbm,
    skv_hbm,
    so_hbm,
    shkv_hbm,
    cq_hbm,
    co_hbm,
    out_ref,
    gains_ref,
    sq,
    skv,
    so,
    shkv,
    wall,
    xg,
    rs,
    ob,
    xs,
    acc,
    qs,
    ctx,
    own_kv,
    halo,
    kc,
    vc,
    sc,
    den,
    oacc,
    load_sem,
    own_sem,
    ag_send,
    ag_recv,
    rs_send,
    rs_recv,
    halo_send,
    halo_recv,
    wz_send,
    wz_recv,
    wx_send,
    wx_recv,
    wy_send,
    wy_recv,
    ws_send,
    ws_recv,
    cz_send,
    cz_recv,
    cx_send,
    cx_recv,
    cs_send,
    cs_recv,
):
    seq = lax.axis_index("seq")
    head = lax.axis_index("head")
    core = rem(seq, 2)
    xp = rem(div(seq, 2), 4)
    zh = div(seq, 8)
    yp = div(head, 2)
    zl = rem(head, 2)

    def seq_at(zz, xx, cc):
        return zz * 8 + xx * 2 + cc

    def head_to(k):
        return rem(yp + div(k, 2), 4) * 2 + rem(zl + rem(k, 2), 2)

    def head_from(k):
        return rem(yp + 4 - div(k, 2), 4) * 2 + rem(zl + rem(k, 2), 2)

    z_to = [rem(zh + d, 4) for d in (1, 2, 3)]
    z_from = [rem(zh + 4 - d, 4) for d in (1, 2, 3)]
    x_to = [rem(xp + d, 4) for d in (1, 2, 3)]
    x_from = [rem(xp + 4 - d, 4) for d in (1, 2, 3)]
    sibling = seq_at(zh, xp, 1 - core)
    following = rem(seq + 1, 32)
    previous = rem(seq + 31, 32)

    def rows_half(h):
        return pl.ds(h * HALF, HALF)

    barrier = pltpu.get_barrier_semaphore()

    def greet(s, h):
        pl.semaphore_signal(barrier, inc=1, device_id=(s, h), device_id_type=MESH)

    for zz in z_to:
        greet(seq_at(zz, xp, core), head)
    for k in range(1, 8):
        greet(seq, head_to(jnp.int32(k)))
    for xx in x_to:
        greet(seq_at(zh, xx, core), head)
    greet(sibling, head)
    greet(following, head)
    greet(previous, head)

    loads = [
        pltpu.make_async_copy(a, b, load_sem.at[i])
        for i, (a, b) in enumerate(
            (
                (tokens_hbm.at[rows_half(0)], xg.at[0, head]),
                (tokens_hbm.at[rows_half(1)], xg.at[1, head]),
                (gains_hbm, gains_ref),
                (skv_hbm, skv),
                (sq_hbm, sq),
                (so_hbm, so),
                (shkv_hbm, shkv),
            )
        )
    ]
    for copy in loads:
        copy.start()

    def piece_source(p):
        return (cq_hbm if p % 2 == 0 else co_hbm).at[p // 2]

    owns = [
        pltpu.make_async_copy(piece_source(p), wall.at[p, zh, xp, core], own_sem.at[p])
        for p in range(6)
    ]
    for copy in owns:
        copy.start()

    with mark("barrier"):
        pl.semaphore_wait(barrier, 16)

    def remote(src, dst, send, recv, s, h):
        return pltpu.make_async_remote_copy(
            src_ref=src, dst_ref=dst, send_sem=send, recv_sem=recv, device_id=(s, h), device_id_type=MESH
        )

    beside_z = yp * 2 + 1 - zl

    def ag_out(h, k, src):
        return remote(src, xg.at[h, head], ag_send.at[h, k], ag_recv.at[h, k], seq, head_to(jnp.int32(k)))

    def ag_pass(h, k):
        part = xg.at[h, beside_z]
        return remote(part, part, ag_send.at[h, k], ag_recv.at[h, k], seq, head_to(jnp.int32(k - 1)))

    def ag_in(h, k):
        return remote(
            xg.at[h, head], xg.at[h, head_from(jnp.int32(k))], ag_send.at[h, k], ag_recv.at[h, k], seq,
            head_to(jnp.int32(k)),
        )

    def ag_start(h, src):
        for k in (1, 2, 6, 4):
            ag_out(h, k, src).start()

    def ag_forward(h):
        with mark("forward"):
            ag_in(h, 1).wait_recv()
            for k in (3, 7, 5):
                ag_pass(h, k).start()

    def ag_near(h):
        for k in (2, 6, 4):
            ag_in(h, k).wait_recv()

    def ag_far(h):
        for k in (3, 7, 5):
            ag_in(h, k).wait_recv()

    def ag_drain(h, src):
        for k in (1, 2, 6, 4):
            ag_out(h, k, src).wait_send()
        for k in (3, 7, 5):
            ag_pass(h, k).wait_send()

    def rs_copy(h, k):
        to = head_to(jnp.int32(k))
        return remote(ob.at[h, to], rs.at[h, k], rs_send.at[h, k], rs_recv.at[h, k], seq, to)

    beside_zh = (z_to[0], z_to[2])
    direct = (3,)

    def wz_copy(p, i, src, dst):
        to = beside_zh[i] if i < 2 else (z_to[1] if p in direct else beside_zh[i - 2])
        return remote(src, dst, wz_send.at[p, i], wz_recv.at[p, i], seq_at(to, xp, core), head)

    def wz_part(p, i, zz):
        if i < 2 or p in direct:
            return wall.at[p, zz, xp, core]
        return wall.at[p, zz, xp, core, pl.ds((i - 2) * (PIECE // 2), PIECE // 2)]

    def wz_out(p, i):
        if i < 2 or p in direct:
            return wz_copy(p, i, piece_source(p), wz_part(p, i, zh))
        part = wz_part(p, i, beside_zh[3 - i])
        return wz_copy(p, i, part, part)

    def wz_in(p, i):
        part = wz_part(p, i, beside_zh[1 - i] if i < 2 else z_to[1])
        return wz_copy(p, i, part, part)

    def wz_steps(p):
        return (0, 1, 2) if p in direct else (0, 1, 2, 3)

    beside = (x_to[0], x_to[2])

    def wx_out(p, i):
        part = wall.at[p, :, xp, core]
        return remote(part, part, wx_send.at[p, i], wx_recv.at[p, i], seq_at(zh, beside[i], core), head)

    def wx_in(p, i):
        part = wall.at[p, :, beside[1 - i], core]
        return remote(part, part, wx_send.at[p, i], wx_recv.at[p, i], seq_at(zh, beside[i], core), head)

    def wy_out(p, i):
        part = wall.at[p, pl.ds(2 * i, 2), beside[1 - i], core]
        return remote(part, part, wy_send.at[p, i], wy_recv.at[p, i], seq_at(zh, beside[i], core), head)

    def wy_in(p, i):
        part = wall.at[p, pl.ds(2 * i, 2), x_to[1], core]
        return remote(part, part, wy_send.at[p, i], wy_recv.at[p, i], seq_at(zh, beside[i], core), head)

    def ws_out(p):
        part = wall.at[p, :, :, core]
        return remote(part, part, ws_send.at[p], ws_recv.at[p], sibling, head)

    def ws_in(p):
        part = wall.at[p, :, :, 1 - core]
        return remote(part, part, ws_send.at[p], ws_recv.at[p], sibling, head)

    def weight_z(p):
        for i in (0, 1, 2) if p in direct else (0, 1):
            wz_out(p, i).start()

    def weight_f(p):
        with mark("weight_f"):
            for i in (0, 1):
                wz_in(p, i).wait_recv()
                wz_out(p, i + 2).start()

    def weight_x(p):
        with mark("weight_x"):
            owns[p].wait()
            for i in (0, 1, 2) if p in direct else (2, 3):
                wz_in(p, i).wait_recv()
            for i in range(2):
                wx_out(p, i).start()

    def weight_y(p):
        with mark("weight_y"):
            for i in range(2):
                wx_in(p, i).wait_recv()
                wy_out(p, i).start()

    def weight_s(p):
        with mark("weight_s"):
            for i in range(2):
                wy_in(p, i).wait_recv()
            ws_out(p).start()

    def weight_wait(p):
        with mark("weight_wait"):
            ws_in(p).wait_recv()

    cache = (kc, vc)

    def cz_part(c, h, zz):
        return cache[c].at[zz, xp, core, rows_half(h)]

    def cz_out(c, h, i):
        part = cz_part(c, h, zh)
        return remote(part, part, cz_send.at[c, h, i], cz_recv.at[c, h, i], seq_at(z_to[i], xp, core), head)

    def cz_in(c, h, i):
        part = cz_part(c, h, z_from[i])
        return remote(part, part, cz_send.at[c, h, i], cz_recv.at[c, h, i], seq_at(z_to[i], xp, core), head)

    def cx_out(c, h, m, i):
        part = cz_part(c, h, rem(zh + 4 - m, 4))
        return remote(part, part, cx_send.at[c, h, m, i], cx_recv.at[c, h, m, i], seq_at(zh, x_to[i], core), head)

    def cx_in(c, h, m, i):
        part = cache[c].at[rem(zh + 4 - m, 4), x_from[i], core, rows_half(h)]
        return remote(part, part, cx_send.at[c, h, m, i], cx_recv.at[c, h, m, i], seq_at(zh, x_to[i], core), head)

    def cs_out(c, h):
        part = cache[c].at[:, :, core, rows_half(h)]
        return remote(part, part, cs_send.at[c, h], cs_recv.at[c, h], sibling, head)

    def cs_in(c, h):
        part = cache[c].at[:, :, 1 - core, rows_half(h)]
        return remote(part, part, cs_send.at[c, h], cs_recv.at[c, h], sibling, head)

    def cols_of(j):
        return pl.ds(pl.multiple_of(j * COLS, 128), COLS)

    def gain(row, j):
        return gains_ref[row : row + 1, cols_of(j)]

    def square_sum(xf):
        sq2 = xf * xf
        return sq2[:, :HEAD] + sq2[:, HEAD : 2 * HEAD] + sq2[:, 2 * HEAD :]

    def row_factor(squares):
        return lax.rsqrt(jnp.sum(squares, axis=1, keepdims=True) / WIDTH + EPSILON)

    def plane(h, zz, row):
        parts, squares = [], 0.0
        for y in range(4):
            j = y * 2 + zz
            xf = xg[h, j].astype(F32)
            squares = squares + square_sum(xf)
            parts.append((xf * gain(row, j)).astype(BF16))
        return jnp.concatenate(parts, axis=1), squares

    def key_value_rows(ref, zz):
        keys = jnp.concatenate([ref[0, cols_of(y * 2 + zz)] for y in range(4)], axis=0)
        values = jnp.concatenate([ref[1, cols_of(y * 2 + zz)] for y in range(4)], axis=0)
        return jnp.concatenate([keys, values], axis=1)

    def piece_rows(p, zz):
        return wall[p, :, pl.ds(zz * 2, 2)].reshape(4 * COLS, COLS)

    def stack_query(h, full, factor):
        scaled = full * (factor * SCORE_SCALE)
        for g in range(GROUP):
            qs[h, g * HALF : (g + 1) * HALF, :] = scaled[:, g * HEAD : (g + 1) * HEAD].astype(BF16)

    def spread_context():
        inv = 1.0 / jnp.sum(den[...], axis=1, keepdims=True)
        c = (oacc[...] * inv).astype(BF16)
        for g in range(GROUP):
            ctx[:, g * HEAD : (g + 1) * HEAD] = c[g * HALF : (g + 1) * HALF, :]

    far = (3, 7, 5, 1)
    near = (4, 2, 6)

    def reduce_out(h, plane_of):
        with mark("rs_out"):
            for zz, ks in ((1 - zl, far), (zl, near)):
                for y, block in enumerate(plane_of(zz)):
                    ob[h, y * 2 + zz] = block.astype(BF16)
                for k in ks:
                    rs_copy(h, k).start()

    def reduce_in(h):
        with mark("rs_in"):
            for k in near + far:
                rs_copy(h, k).wait_recv()
            total = xs[h] + ob[h, head].astype(F32)
            for k in near + far:
                total = total + rs[h, k].astype(F32)
        return total

    def rs_drain(h):
        for k in near + far:
            rs_copy(h, k).wait_send()

    def own_part(h):
        return xg.at[h, head]

    for h in range(2):
        ag_start(h, tokens_hbm.at[rows_half(h)])
    weight_z(0)
    for h in range(2):
        ag_forward(h)
    weight_z(1)
    for copy in loads[:5]:
        copy.wait()

    def halo_of(h):
        return remote(
            own_kv.at[:, rows_half(h)], halo.at[:, rows_half(h)], halo_send.at[h], halo_recv.at[h], following, head
        )

    for h in range(2):
        xs[h] = xg[h, head].astype(F32)
        with mark("ag0"):
            ag_near(h)
            hb, squares = plane(h, zl, 0)
            acc[:, COLS:] = dot(hb, key_value_rows(skv, zl))
            acc[:, :COLS] = dot(hb, jnp.concatenate([sq[cols_of(y * 2 + zl)] for y in range(4)], axis=0))
            ag_far(h)
            hb, more = plane(h, 1 - zl, 0)
            factor = row_factor(squares + more)
            kv = (acc[:, COLS:] + dot(hb, key_value_rows(skv, 1 - zl))) * factor
            own_kv[0, rows_half(h)] = kv[:, :HEAD].astype(BF16)
            own_kv[1, rows_half(h)] = kv[:, HEAD:].astype(BF16)
            halo_of(h).start()
            full = acc[:, :COLS] + dot(
                hb, jnp.concatenate([sq[cols_of(y * 2 + 1 - zl)] for y in range(4)], axis=0)
            )
            stack_query(h, full, factor)
        weight_f(h)
    for h in range(2):
        ag_drain(h, tokens_hbm.at[rows_half(h)])

    col = lax.broadcasted_iota(jnp.int32, (1, 2 * ROWS), 1)
    loads[5].wait()
    with mark("halo"):
        for h in range(2):
            halo_of(h).wait_recv()
    for h in range(2):
        row = lax.broadcasted_iota(jnp.int32, (HALF, 1), 0) + h * HALF
        offset = row + ROWS - col
        present = (offset >= 0) & (col >= jnp.where(seq == 0, ROWS, 0))
        with mark("self_attn"):
            for g in range(GROUP):
                here = slice(g * HALF, (g + 1) * HALF)
                qg = qs[h, here, :]
                score = jnp.concatenate([dot_t(qg, halo[0]), dot_t(qg, own_kv[0])], axis=1)
                score = jnp.where(present & (offset < window_ref[g]), score, MASKED)
                top = jnp.max(score, axis=1, keepdims=True)
                weights = jnp.exp2(score - top)
                den[here, :] = weights[:, :ROWS] + weights[:, ROWS:]
                wb = weights.astype(BF16)
                oacc[here, :] = dot(wb[:, :ROWS], halo[1]) + dot(wb[:, ROWS:], own_kv[1])
            spread_context()
        cvals = ctx[...]
        reduce_out(h, lambda zz, cvals=cvals: [dot(cvals, so[:, cols_of(y * 2 + zz)]) for y in range(4)])
        weight_x(h)
    for h in range(2):
        total = reduce_in(h)
        xs[h] = total
        xg[h, head] = total.astype(BF16)
        ag_start(h, own_part(h))
        if h == 0:
            weight_z(2)
            ag_forward(0)
            weight_y(0)
    loads[6].wait()

    factors = []
    for h in range(2):
        with mark("ag1"):
            ag_near(h)
            hb, squares = plane(h, zl, 1)
            acc[:, COLS:] = dot(hb, key_value_rows(shkv, zl))
            if h == 0:
                ag_forward(1)
            ag_far(h)
            hb, more = plane(h, 1 - zl, 1)
            factor = row_factor(squares + more)
            kv = (acc[:, COLS:] + dot(hb, key_value_rows(shkv, 1 - zl))) * factor
        factors.append(factor)
        for c in range(2):
            cache[c][zh, xp, core, rows_half(h)] = kv[:, c * HEAD : (c + 1) * HEAD].astype(BF16)
            for i in range(3):
                cz_out(c, h, i).start()
            for i in range(3):
                cx_out(c, h, 0, i).start()
        if h == 0:
            weight_f(2)
            weight_y(1)
    weight_s(0)
    weight_z(3)
    weight_z(4)
    with mark("cache_z"):
        for h in range(2):
            for c in range(2):
                for m in (1, 2, 3):
                    cz_in(c, h, m - 1).wait_recv()
                    for i in range(3):
                        cx_out(c, h, m, i).start()
    weight_x(2)
    weight_z(5)
    weight_s(1)
    weight_wait(0)
    for h in range(2):
        rs_drain(h)
        with mark("q0"):
            full = 0.0
            for zz in (0, 1):
                hb, _ = plane(h, zz, 2)
                full = full + dot(hb, piece_rows(0, zz))
        stack_query(h, full, factors[h])
        ag_drain(h, own_part(h))
    with mark("cache_x"):
        for h in range(2):
            for c in range(2):
                for m in range(4):
                    for i in range(3):
                        cx_in(c, h, m, i).wait_recv()
                cs_out(c, h).start()
    weight_x(3)
    weight_f(4)
    with mark("cache_s"):
        for h in range(2):
            for c in range(2):
                cs_in(c, h).wait_recv()

    half_row = rem(lax.broadcasted_iota(jnp.int32, (GROUP * HALF, 1), 0), HALF)
    causal_col = jnp.where(col < ROWS, col, -1)

    for section in range(3):
        for h in range(2):
            if section > 0:
                if section == 1 and h == 0:
                    weight_s(3)
                if h == 0:
                    weight_wait(2 * section)
                with mark("ag"):
                    ag_near(h)
                    hb, squares = plane(h, zl, 2 + section)
                    acc[:, :COLS] = dot(hb, piece_rows(2 * section, zl))
                    ag_far(h)
                    hb, more = plane(h, 1 - zl, 2 + section)
                    full = acc[:, :COLS] + dot(hb, piece_rows(2 * section, 1 - zl))
                    stack_query(h, full, row_factor(squares + more))

            qv = qs[h]

            def pick(ref, i, section=section):
                n = jnp.maximum(blocks_ref[section, 0, i], 0)
                return ref[div(n, 8), rem(div(n, 2), 4), rem(n, 2)]

            with mark("score"):
                best = None
                for i in range(8):
                    keys = jnp.concatenate([pick(kc, 2 * i), pick(kc, 2 * i + 1)], axis=0)
                    t = dot_t(qv, keys)
                    low = jnp.where(blocks_ref[section, 0, 2 * i] >= 0, 0.0, MASKED)
                    high = jnp.where(blocks_ref[section, 0, 2 * i + 1] >= 0, 0.0, MASKED)
                    if i == 0:
                        t = jnp.where(causal_col <= half_row + h * HALF, t, MASKED)
                    t = t + jnp.where(col < ROWS, low, high)
                    sc[i] = t
                    pair = jnp.maximum(t[:, :HEAD], t[:, HEAD:])
                    best = pair if best is None else jnp.maximum(best, pair)
                top = jnp.max(best, axis=1, keepdims=True)
            if section > 0:
                if h == 0:
                    ag_forward(1)
                ag_drain(h, own_part(h))

            with mark("value"):
                dens, outs = None, None
                for i in range(8):
                    weights = jnp.exp2(sc[i] - top)
                    part = weights[:, :HEAD] + weights[:, HEAD:]
                    dens = part if dens is None else dens + part
                    values = jnp.concatenate([pick(vc, 2 * i), pick(vc, 2 * i + 1)], axis=0)
                    part = dot(weights.astype(BF16), values)
                    outs = part if outs is None else outs + part
                den[...] = dens
                oacc[...] = outs
            spread_context()
            if section == 0 and h == 0:
                weight_f(5)
            if h == 0:
                weight_wait(2 * section + 1)
            cvals = ctx[...]
            if section > 0:
                rs_drain(h)

            def plane_of(zz, cvals=cvals, section=section):
                wide = dot_t(cvals, piece_rows(2 * section + 1, zz))
                return [wide[:, y * COLS : (y + 1) * COLS] for y in range(4)]

            reduce_out(h, plane_of)
            if section == 0:
                weight_y(2 + h)
            elif section == 1:
                weight_y(4 + h)
        for h in range(2):
            total = reduce_in(h)
            if section < 2:
                xs[h] = total
                xg[h, head] = total.astype(BF16)
                ag_start(h, own_part(h))
                if section == 0 and h == 0:
                    weight_x(4)
                if h == 0:
                    ag_forward(0)
            else:
                out_ref[rows_half(h), :] = total
            if section == 0 and h == 0:
                weight_s(2)
            elif section == 0 and h == 1:
                weight_x(5)
            elif section == 1:
                weight_s(4 + h)
    for h in range(2):
        rs_drain(h)

    for h in range(2):
        halo_of(h).wait_send()
    for p in range(6):
        for i in wz_steps(p):
            wz_out(p, i).wait_send()
        for i in range(2):
            wx_out(p, i).wait_send()
            wy_out(p, i).wait_send()
        ws_out(p).wait_send()
    for c in range(2):
        for h in range(2):
            for i in range(3):
                cz_out(c, h, i).wait_send()
                for m in range(4):
                    cx_out(c, h, m, i).wait_send()
            cs_out(c, h).wait_send()


def body(
    tokens,
    norm_gains,
    window,
    self_query,
    self_key_value,
    self_output,
    shared_key_value,
    cross_query,
    cross_output,
    key_blocks,
):
    vmem = pl.BlockSpec(memory_space=pltpu.VMEM)
    smem = pl.BlockSpec(memory_space=pltpu.SMEM)
    hbm = pl.BlockSpec(memory_space=pl.ANY)
    dma = pltpu.SemaphoreType.DMA
    return pl.pallas_call(
        kernel,
        out_shape=jax.ShapeDtypeStruct((ROWS, COLS), F32),
        in_specs=[smem, smem] + [hbm] * 8,
        out_specs=vmem,
        scratch_shapes=[
            pltpu.VMEM((5, WIDTH), F32),
            pltpu.VMEM((WIDTH, COLS), BF16),
            pltpu.VMEM((2, WIDTH, HEAD), BF16),
            pltpu.VMEM((COLS, WIDTH), BF16),
            pltpu.VMEM((2, WIDTH, HEAD), BF16),
            pltpu.VMEM((6, 4, 4, 2, PIECE, COLS), BF16),
            pltpu.VMEM((2, 8, HALF, COLS), BF16),
            pltpu.VMEM((2, 8, HALF, COLS), BF16),
            pltpu.VMEM((2, 8, HALF, COLS), BF16),
            pltpu.VMEM((2, HALF, COLS), F32),
            pltpu.VMEM((HALF, COLS + 2 * HEAD), F32),
            pltpu.VMEM((2, GROUP * HALF, HEAD), BF16),
            pltpu.VMEM((HALF, COLS), BF16),
            pltpu.VMEM((2, ROWS, HEAD), BF16),
            pltpu.VMEM((2, ROWS, HEAD), BF16),
            pltpu.VMEM((4, 4, 2, ROWS, HEAD), BF16),
            pltpu.VMEM((4, 4, 2, ROWS, HEAD), BF16),
            pltpu.VMEM((8, GROUP * HALF, 2 * HEAD), F32),
            pltpu.VMEM((GROUP * HALF, HEAD), F32),
            pltpu.VMEM((GROUP * HALF, HEAD), F32),
            dma((7,)),
            dma((6,)),
            dma((2, 8)),
            dma((2, 8)),
            dma((2, 8)),
            dma((2, 8)),
            dma((2,)),
            dma((2,)),
            dma((6, 4)),
            dma((6, 4)),
            dma((6, 2)),
            dma((6, 2)),
            dma((6, 2)),
            dma((6, 2)),
            dma((6,)),
            dma((6,)),
            dma((2, 2, 3)),
            dma((2, 2, 3)),
            dma((2, 2, 4, 3)),
            dma((2, 2, 4, 3)),
            dma((2, 2)),
            dma((2, 2)),
        ],
        compiler_params=pltpu.CompilerParams(
            collective_id=0, has_side_effects=True, vmem_limit_bytes=60 * 1024 * 1024
        ),
        name="window",
    )(
        window,
        key_blocks,
        tokens,
        norm_gains,
        self_query,
        self_key_value,
        self_output,
        shared_key_value,
        cross_query,
        jnp.swapaxes(cross_output, 1, 2),
    )


def solution(mesh):
    placed = (
        P("seq", "head"),
        P(),
        P("head"),
        P(None, "head"),
        P(None, None, "head"),
        P("head", None),
        P(None, None, "head"),
        P(None, "seq", "head"),
        P(None, "head", "seq"),
        P(None, "seq", None),
    )
    return jax.shard_map(
        body, mesh=mesh, in_specs=placed, out_specs=P("seq", "head"), check_vma=False
    )
```

```python
import math

import jax
import jax.numpy as jnp
from jax import lax
from jax.experimental import pallas as pl
from jax.experimental.pallas import tpu as pltpu
from jax.sharding import PartitionSpec as P

MESH = pl.DeviceIdType.MESH
EPSILON = 1e-06
MASKED = -1e30
F32 = jnp.float32
BF16 = jnp.bfloat16
WIDTH = 3072
ROWS = 128
COLS = 384
HEAD = 128
GROUP = 3
PIECE = 96
HALF = 64
SCORE_SCALE = HEAD ** (-0.5) * math.log2(math.e)


mark = jax.named_scope


def rem(a, b):
    return lax.rem(a, jnp.int32(b))


def div(a, b):
    return lax.div(a, jnp.int32(b))


def dot(a, b):
    return jnp.dot(a, b, preferred_element_type=F32)


def dot_t(a, b):
    return lax.dot_general(a, b, (((1,), (1,)), ((), ())), preferred_element_type=F32)


def kernel(
    window_ref,
    blocks_ref,
    tokens_hbm,
    gains_hbm,
    sq_hbm,
    skv_hbm,
    so_hbm,
    shkv_hbm,
    cq_hbm,
    co_hbm,
    out_ref,
    gains_ref,
    sq,
    skv,
    so,
    shkv,
    wall,
    xg,
    rs,
    ob,
    xs,
    acc,
    qs,
    ctx,
    own_kv,
    halo,
    kc,
    vc,
    sc,
    den,
    oacc,
    load_sem,
    own_sem,
    ag_send,
    ag_recv,
    rs_send,
    rs_recv,
    halo_send,
    halo_recv,
    wz_send,
    wz_recv,
    wx_send,
    wx_recv,
    wy_send,
    wy_recv,
    ws_send,
    ws_recv,
    cz_send,
    cz_recv,
    cx_send,
    cx_recv,
    cs_send,
    cs_recv,
):
    seq = lax.axis_index("seq")
    head = lax.axis_index("head")
    core = rem(seq, 2)
    xp = rem(div(seq, 2), 4)
    zh = div(seq, 8)
    yp = div(head, 2)
    zl = rem(head, 2)

    def seq_at(zz, xx, cc):
        return zz * 8 + xx * 2 + cc

    def head_to(k):
        return rem(yp + div(k, 2), 4) * 2 + rem(zl + rem(k, 2), 2)

    def head_from(k):
        return rem(yp + 4 - div(k, 2), 4) * 2 + rem(zl + rem(k, 2), 2)

    z_to = [rem(zh + d, 4) for d in (1, 2, 3)]
    z_from = [rem(zh + 4 - d, 4) for d in (1, 2, 3)]
    x_to = [rem(xp + d, 4) for d in (1, 2, 3)]
    x_from = [rem(xp + 4 - d, 4) for d in (1, 2, 3)]
    sibling = seq_at(zh, xp, 1 - core)
    following = rem(seq + 1, 32)
    previous = rem(seq + 31, 32)

    def rows_half(h):
        return pl.ds(h * HALF, HALF)

    barrier = pltpu.get_barrier_semaphore()

    def greet(s, h):
        pl.semaphore_signal(barrier, inc=1, device_id=(s, h), device_id_type=MESH)

    for zz in z_to:
        greet(seq_at(zz, xp, core), head)
    for k in range(1, 8):
        greet(seq, head_to(jnp.int32(k)))
    for xx in x_to:
        greet(seq_at(zh, xx, core), head)
    greet(sibling, head)
    greet(following, head)
    greet(previous, head)

    loads = [
        pltpu.make_async_copy(a, b, load_sem.at[i])
        for i, (a, b) in enumerate(
            (
                (tokens_hbm.at[rows_half(0)], xg.at[0, head]),
                (tokens_hbm.at[rows_half(1)], xg.at[1, head]),
                (gains_hbm, gains_ref),
                (skv_hbm, skv),
                (sq_hbm, sq),
                (so_hbm, so),
                (shkv_hbm, shkv),
            )
        )
    ]
    for copy in loads:
        copy.start()

    def piece_source(p):
        return (cq_hbm if p % 2 == 0 else co_hbm).at[p // 2]

    owns = [
        pltpu.make_async_copy(piece_source(p), wall.at[p, zh, xp, core], own_sem)
        for p in range(6)
    ]
    for copy in owns:
        copy.start()

    with mark("barrier"):
        pl.semaphore_wait(barrier, 16)

    def remote(src, dst, send, recv, s, h):
        return pltpu.make_async_remote_copy(
            src_ref=src, dst_ref=dst, send_sem=send, recv_sem=recv, device_id=(s, h), device_id_type=MESH
        )

    def take(ref, sem):
        pltpu.make_async_copy(ref, ref, sem).wait()

    beside_z = yp * 2 + 1 - zl

    def ag_slot(k):
        return 0 if k == 1 else 1 + k % 2

    def ag_out(h, k, src):
        return remote(
            src, xg.at[h, head], ag_send.at[h], ag_recv.at[h, ag_slot(k)], seq, head_to(jnp.int32(k))
        )

    def ag_pass(h, k):
        part = xg.at[h, beside_z]
        return remote(part, part, ag_send.at[h], ag_recv.at[h, ag_slot(k)], seq, head_to(jnp.int32(k - 1)))

    def ag_start(h, src):
        for k in (1, 2, 6, 4):
            ag_out(h, k, src).start()

    def ag_forward(h):
        with mark("forward"):
            take(xg.at[h, 0], ag_recv.at[h, 0])
            for k in (3, 7, 5):
                ag_pass(h, k).start()

    def ag_near(h):
        take(xg.at[h, pl.ds(0, 3)], ag_recv.at[h, 1])

    def ag_far(h):
        take(xg.at[h, pl.ds(0, 3)], ag_recv.at[h, 2])

    def ag_drain(h):
        take(xg.at[h, pl.ds(0, 7)], ag_send.at[h])

    def rs_copy(h, k):
        to = head_to(jnp.int32(k))
        return remote(ob.at[h, to], rs.at[h, k], rs_send.at[h], rs_recv.at[h], seq, to)

    beside_zh = (z_to[0], z_to[2])
    direct = (3,)

    def wz_copy(p, i, src, dst):
        to = beside_zh[i] if i < 2 else (z_to[1] if p in direct else beside_zh[i - 2])
        step = i // 2 if p not in direct else 0
        return remote(src, dst, wz_send, wz_recv.at[p, step], seq_at(to, xp, core), head)

    def wz_part(p, i, zz):
        if i < 2 or p in direct:
            return wall.at[p, zz, xp, core]
        return wall.at[p, zz, xp, core, pl.ds((i - 2) * (PIECE // 2), PIECE // 2)]

    def wz_out(p, i):
        if i < 2 or p in direct:
            return wz_copy(p, i, piece_source(p), wz_part(p, i, zh))
        part = wz_part(p, i, beside_zh[3 - i])
        return wz_copy(p, i, part, part)

    beside = (x_to[0], x_to[2])

    def wx_out(p, i):
        part = wall.at[p, :, xp, core]
        return remote(part, part, wx_send, wx_recv.at[p], seq_at(zh, beside[i], core), head)

    def wy_out(p, i):
        part = wall.at[p, pl.ds(2 * i, 2), beside[1 - i], core]
        return remote(part, part, wy_send, wy_recv.at[p], seq_at(zh, beside[i], core), head)

    def ws_out(p):
        part = wall.at[p, :, :, core]
        return remote(part, part, ws_send, ws_recv.at[p], sibling, head)

    def weight_z(p):
        for i in (0, 1, 2) if p in direct else (0, 1):
            wz_out(p, i).start()

    def weight_f(p):
        with mark("weight_f"):
            take(wall.at[p, 0, 0], wz_recv.at[p, 0])
            for i in (0, 1):
                wz_out(p, i + 2).start()

    def weight_x(p):
        with mark("weight_x"):
            if p in direct:
                take(wall.at[p, pl.ds(0, 3), 0, 0], wz_recv.at[p, 0])
            else:
                take(wall.at[p, 0, 0, 0], wz_recv.at[p, 1])
            for i in range(2):
                wx_out(p, i).start()

    def weight_y(p):
        with mark("weight_y"):
            take(wall.at[p, :, 0], wx_recv.at[p])
            for i in range(2):
                wy_out(p, i).start()

    def weight_s(p):
        with mark("weight_s"):
            take(wall.at[p, 0, pl.ds(0, 2)], wy_recv.at[p])
            ws_out(p).start()

    def weight_wait(p):
        with mark("weight_wait"):
            take(wall.at[p, :, :, 0], ws_recv.at[p])

    cache = (kc, vc)

    def cz_part(c, h, zz):
        return cache[c].at[zz, xp, core, rows_half(h)]

    def cz_out(c, h, i):
        part = cz_part(c, h, zh)
        return remote(part, part, cz_send, cz_recv.at[c, h, i], seq_at(z_to[i], xp, core), head)

    def cz_in(c, h, i):
        part = cz_part(c, h, z_from[i])
        return remote(part, part, cz_send, cz_recv.at[c, h, i], seq_at(z_to[i], xp, core), head)

    def cx_out(c, h, m, i):
        part = cz_part(c, h, rem(zh + 4 - m, 4))
        return remote(part, part, cx_send, cx_recv.at[c, h], seq_at(zh, x_to[i], core), head)

    def cs_out(c, h):
        part = cache[c].at[:, :, core, rows_half(h)]
        return remote(part, part, cs_send, cs_recv.at[c], sibling, head)

    def cols_of(j):
        return pl.ds(pl.multiple_of(j * COLS, 128), COLS)

    def gain(row, j):
        return gains_ref[row : row + 1, cols_of(j)]

    def square_sum(xf):
        sq2 = xf * xf
        return sq2[:, :HEAD] + sq2[:, HEAD : 2 * HEAD] + sq2[:, 2 * HEAD :]

    def row_factor(squares):
        return lax.rsqrt(jnp.sum(squares, axis=1, keepdims=True) / WIDTH + EPSILON)

    def plane(h, zz, row):
        parts, squares = [], 0.0
        for y in range(4):
            j = y * 2 + zz
            xf = xg[h, j].astype(F32)
            squares = squares + square_sum(xf)
            parts.append((xf * gain(row, j)).astype(BF16))
        return jnp.concatenate(parts, axis=1), squares

    def key_value_rows(ref, zz):
        keys = jnp.concatenate([ref[0, cols_of(y * 2 + zz)] for y in range(4)], axis=0)
        values = jnp.concatenate([ref[1, cols_of(y * 2 + zz)] for y in range(4)], axis=0)
        return jnp.concatenate([keys, values], axis=1)

    def piece_rows(p, zz):
        return wall[p, :, pl.ds(zz * 2, 2)].reshape(4 * COLS, COLS)

    def stack_query(h, full, factor):
        scaled = full * (factor * SCORE_SCALE)
        for g in range(GROUP):
            qs[h, g * HALF : (g + 1) * HALF, :] = scaled[:, g * HEAD : (g + 1) * HEAD].astype(BF16)

    def spread_context():
        inv = 1.0 / jnp.sum(den[...], axis=1, keepdims=True)
        c = (oacc[...] * inv).astype(BF16)
        for g in range(GROUP):
            ctx[:, g * HEAD : (g + 1) * HEAD] = c[g * HALF : (g + 1) * HALF, :]

    far = (3, 7, 5, 1)
    near = (4, 2, 6)

    def reduce_out(h, plane_of):
        with mark("rs_out"):
            for zz, ks in ((1 - zl, far), (zl, near)):
                for y, block in enumerate(plane_of(zz)):
                    ob[h, y * 2 + zz] = block.astype(BF16)
                for k in ks:
                    rs_copy(h, k).start()

    def reduce_in(h):
        with mark("rs_in"):
            take(rs.at[h, pl.ds(1, 7)], rs_recv.at[h])
            total = xs[h] + ob[h, head].astype(F32)
            for k in near + far:
                total = total + rs[h, k].astype(F32)
        return total

    def rs_drain(h):
        take(ob.at[h, pl.ds(0, 7)], rs_send.at[h])

    def own_part(h):
        return xg.at[h, head]

    for h in range(2):
        ag_start(h, tokens_hbm.at[rows_half(h)])
    weight_z(0)
    for h in range(2):
        ag_forward(h)
    weight_z(1)
    for copy in loads[:5]:
        copy.wait()

    def halo_of(h):
        return remote(
            own_kv.at[:, rows_half(h)], halo.at[:, rows_half(h)], halo_send, halo_recv, following, head
        )

    for h in range(2):
        xs[h] = xg[h, head].astype(F32)
        with mark("ag0"):
            ag_near(h)
            hb, squares = plane(h, zl, 0)
            acc[:, COLS:] = dot(hb, key_value_rows(skv, zl))
            acc[:, :COLS] = dot(hb, jnp.concatenate([sq[cols_of(y * 2 + zl)] for y in range(4)], axis=0))
            ag_far(h)
            hb, more = plane(h, 1 - zl, 0)
            factor = row_factor(squares + more)
            kv = (acc[:, COLS:] + dot(hb, key_value_rows(skv, 1 - zl))) * factor
            own_kv[0, rows_half(h)] = kv[:, :HEAD].astype(BF16)
            own_kv[1, rows_half(h)] = kv[:, HEAD:].astype(BF16)
            halo_of(h).start()
            full = acc[:, :COLS] + dot(
                hb, jnp.concatenate([sq[cols_of(y * 2 + 1 - zl)] for y in range(4)], axis=0)
            )
            stack_query(h, full, factor)
        weight_f(h)
    for h in range(2):
        ag_drain(h)

    col = lax.broadcasted_iota(jnp.int32, (1, 2 * ROWS), 1)
    loads[5].wait()
    with mark("halo"):
        take(halo, halo_recv)
    for h in range(2):
        row = lax.broadcasted_iota(jnp.int32, (HALF, 1), 0) + h * HALF
        offset = row + ROWS - col
        present = (offset >= 0) & (col >= jnp.where(seq == 0, ROWS, 0))
        with mark("self_attn"):
            for g in range(GROUP):
                here = slice(g * HALF, (g + 1) * HALF)
                qg = qs[h, here, :]
                score = jnp.concatenate([dot_t(qg, halo[0]), dot_t(qg, own_kv[0])], axis=1)
                score = jnp.where(present & (offset < window_ref[g]), score, MASKED)
                top = jnp.max(score, axis=1, keepdims=True)
                weights = jnp.exp2(score - top)
                den[here, :] = weights[:, :ROWS] + weights[:, ROWS:]
                wb = weights.astype(BF16)
                oacc[here, :] = dot(wb[:, :ROWS], halo[1]) + dot(wb[:, ROWS:], own_kv[1])
            spread_context()
        cvals = ctx[...]
        reduce_out(h, lambda zz, cvals=cvals: [dot(cvals, so[:, cols_of(y * 2 + zz)]) for y in range(4)])
        if h == 0:
            take(wall.at[:, 0, 0, 0], own_sem)
        weight_x(h)
    for h in range(2):
        total = reduce_in(h)
        xs[h] = total
        xg[h, head] = total.astype(BF16)
        ag_start(h, own_part(h))
        if h == 0:
            weight_z(2)
            ag_forward(0)
            weight_y(0)
        else:
            weight_z(4)
    loads[6].wait()

    factors = []
    for h in range(2):
        with mark("ag1"):
            ag_near(h)
            hb, squares = plane(h, zl, 1)
            acc[:, COLS:] = dot(hb, key_value_rows(shkv, zl))
            if h == 0:
                ag_forward(1)
            ag_far(h)
            hb, more = plane(h, 1 - zl, 1)
            factor = row_factor(squares + more)
            kv = (acc[:, COLS:] + dot(hb, key_value_rows(shkv, 1 - zl))) * factor
        factors.append(factor)
        for c in range(2):
            cache[c][zh, xp, core, rows_half(h)] = kv[:, c * HEAD : (c + 1) * HEAD].astype(BF16)
            for i in range(3):
                cz_out(c, h, i).start()
            for i in range(3):
                cx_out(c, h, 0, i).start()
        if h == 0:
            weight_y(1)
    weight_f(2)
    weight_f(4)
    weight_s(0)
    weight_z(3)
    weight_z(5)
    with mark("cache_z"):
        for h in range(2):
            for c in range(2):
                for m in (1, 2, 3):
                    cz_in(c, h, m - 1).wait_recv()
                    for i in range(3):
                        cx_out(c, h, m, i).start()
    weight_x(2)
    weight_s(1)
    weight_wait(0)
    for h in range(2):
        rs_drain(h)
        with mark("q0"):
            full = 0.0
            for zz in (0, 1):
                hb, _ = plane(h, zz, 2)
                full = full + dot(hb, piece_rows(0, zz))
        stack_query(h, full, factors[h])
        ag_drain(h)
    with mark("cache_x"):
        for h in range(2):
            for c in range(2):
                take(cache[c].at[:, pl.ds(0, 3), 0, rows_half(0)], cx_recv.at[c, h])
                cs_out(c, h).start()
    with mark("cache_s"):
        for c in range(2):
            take(cache[c].at[:, :, 0], cs_recv.at[c])

    half_row = rem(lax.broadcasted_iota(jnp.int32, (GROUP * HALF, 1), 0), HALF)
    causal_col = jnp.where(col < ROWS, col, -1)

    for section in range(3):
        for h in range(2):
            if section > 0:
                if h == 0:
                    weight_wait(2 * section)
                with mark("ag"):
                    ag_near(h)
                    hb, squares = plane(h, zl, 2 + section)
                    acc[:, :COLS] = dot(hb, piece_rows(2 * section, zl))
                    if h == 0:
                        if section == 1:
                            weight_x(5)
                        ag_forward(1)
                        if section == 1:
                            weight_s(3)
                    ag_far(h)
                    hb, more = plane(h, 1 - zl, 2 + section)
                    full = acc[:, :COLS] + dot(hb, piece_rows(2 * section, 1 - zl))
                    stack_query(h, full, row_factor(squares + more))

            qv = qs[h]

            def pick(ref, i, section=section):
                n = jnp.maximum(blocks_ref[section, 0, i], 0)
                return ref[div(n, 8), rem(div(n, 2), 4), rem(n, 2)]

            with mark("score"):
                best = None
                for i in range(8):
                    keys = jnp.concatenate([pick(kc, 2 * i), pick(kc, 2 * i + 1)], axis=0)
                    t = dot_t(qv, keys)
                    low = jnp.where(blocks_ref[section, 0, 2 * i] >= 0, 0.0, MASKED)
                    high = jnp.where(blocks_ref[section, 0, 2 * i + 1] >= 0, 0.0, MASKED)
                    if i == 0:
                        t = jnp.where(causal_col <= half_row + h * HALF, t, MASKED)
                    t = t + jnp.where(col < ROWS, low, high)
                    sc[i] = t
                    pair = jnp.maximum(t[:, :HEAD], t[:, HEAD:])
                    best = pair if best is None else jnp.maximum(best, pair)
                top = jnp.max(best, axis=1, keepdims=True)
            if section > 0:
                ag_drain(h)

            with mark("value"):
                dens, outs = None, None
                for i in range(8):
                    weights = jnp.exp2(sc[i] - top)
                    part = weights[:, :HEAD] + weights[:, HEAD:]
                    dens = part if dens is None else dens + part
                    values = jnp.concatenate([pick(vc, 2 * i), pick(vc, 2 * i + 1)], axis=0)
                    part = dot(weights.astype(BF16), values)
                    outs = part if outs is None else outs + part
                den[...] = dens
                oacc[...] = outs
            spread_context()
            if h == 0:
                weight_wait(2 * section + 1)
            cvals = ctx[...]
            if section > 0:
                rs_drain(h)

            def plane_of(zz, cvals=cvals, section=section):
                wide = dot_t(cvals, piece_rows(2 * section + 1, zz))
                return [wide[:, y * COLS : (y + 1) * COLS] for y in range(4)]

            reduce_out(h, plane_of)
            if section == 0 and h == 0:
                weight_x(3)
            elif section == 0:
                weight_y(2)
            elif section == 1:
                weight_y(4 + h)
        for h in range(2):
            total = reduce_in(h)
            if section < 2:
                xs[h] = total
                xg[h, head] = total.astype(BF16)
                ag_start(h, own_part(h))
                if section == 0 and h == 0:
                    weight_f(5)
                    weight_y(3)
                    weight_x(4)
                if h == 0:
                    ag_forward(0)
            else:
                out_ref[rows_half(h), :] = total
            if section == 0 and h == 1:
                weight_s(2)
            elif section == 1:
                weight_s(4 + h)
    with mark("tail"):
        for h in range(2):
            rs_drain(h)

    take(own_kv, halo_send)
    take(wall.at[pl.ds(0, 3), pl.ds(0, 3), 0], wz_send)
    take(wall.at[:, :, 0], wx_send)
    take(wall.at[:, pl.ds(0, 2), 0], wy_send)
    take(wall.at[:, :, :, 0], ws_send)
    take(kc.at[pl.ds(0, 3), 0], cz_send)
    take(kc.at[pl.ds(0, 3)], cx_send)
    take(kc, cs_send)


def body(
    tokens,
    norm_gains,
    window,
    self_query,
    self_key_value,
    self_output,
    shared_key_value,
    cross_query,
    cross_output,
    key_blocks,
):
    vmem = pl.BlockSpec(memory_space=pltpu.VMEM)
    smem = pl.BlockSpec(memory_space=pltpu.SMEM)
    hbm = pl.BlockSpec(memory_space=pl.ANY)
    dma = pltpu.SemaphoreType.DMA
    return pl.pallas_call(
        kernel,
        out_shape=jax.ShapeDtypeStruct((ROWS, COLS), F32),
        in_specs=[smem, smem] + [hbm] * 8,
        out_specs=vmem,
        scratch_shapes=[
            pltpu.VMEM((5, WIDTH), F32),
            pltpu.VMEM((WIDTH, COLS), BF16),
            pltpu.VMEM((2, WIDTH, HEAD), BF16),
            pltpu.VMEM((COLS, WIDTH), BF16),
            pltpu.VMEM((2, WIDTH, HEAD), BF16),
            pltpu.VMEM((6, 4, 4, 2, PIECE, COLS), BF16),
            pltpu.VMEM((2, 8, HALF, COLS), BF16),
            pltpu.VMEM((2, 8, HALF, COLS), BF16),
            pltpu.VMEM((2, 8, HALF, COLS), BF16),
            pltpu.VMEM((2, HALF, COLS), F32),
            pltpu.VMEM((HALF, COLS + 2 * HEAD), F32),
            pltpu.VMEM((2, GROUP * HALF, HEAD), BF16),
            pltpu.VMEM((HALF, COLS), BF16),
            pltpu.VMEM((2, ROWS, HEAD), BF16),
            pltpu.VMEM((2, ROWS, HEAD), BF16),
            pltpu.VMEM((4, 4, 2, ROWS, HEAD), BF16),
            pltpu.VMEM((4, 4, 2, ROWS, HEAD), BF16),
            pltpu.VMEM((8, GROUP * HALF, 2 * HEAD), F32),
            pltpu.VMEM((GROUP * HALF, HEAD), F32),
            pltpu.VMEM((GROUP * HALF, HEAD), F32),
            dma((7,)),
            dma,
            dma((2,)),
            dma((2, 3)),
            dma((2,)),
            dma((2,)),
            dma,
            dma,
            dma,
            dma((6, 2)),
            dma,
            dma((6,)),
            dma,
            dma((6,)),
            dma,
            dma((6,)),
            dma,
            dma((2, 2, 3)),
            dma,
            dma((2, 2)),
            dma,
            dma((2,)),
        ],
        compiler_params=pltpu.CompilerParams(
            collective_id=0, has_side_effects=True, vmem_limit_bytes=60 * 1024 * 1024
        ),
        name="window",
    )(
        window,
        key_blocks,
        tokens,
        norm_gains,
        self_query,
        self_key_value,
        self_output,
        shared_key_value,
        cross_query,
        jnp.swapaxes(cross_output, 1, 2),
    )


def solution(mesh):
    placed = (
        P("seq", "head"),
        P(),
        P("head"),
        P(None, "head"),
        P(None, None, "head"),
        P("head", None),
        P(None, None, "head"),
        P(None, "seq", "head"),
        P(None, "head", "seq"),
        P(None, "seq", None),
    )
    return jax.shard_map(
        body, mesh=mesh, in_specs=placed, out_specs=P("seq", "head"), check_vma=False
    )
```

```python
import math

import jax
import jax.numpy as jnp
from jax import lax
from jax.experimental import pallas as pl
from jax.experimental.pallas import tpu as pltpu
from jax.sharding import PartitionSpec as P

MESH = pl.DeviceIdType.MESH
EPSILON = 1e-06
MASKED = -1e30
F32 = jnp.float32
BF16 = jnp.bfloat16
WIDTH = 3072
ROWS = 128
COLS = 384
HEAD = 128
GROUP = 3
PIECE = 96
HALF = 64
SCORE_SCALE = HEAD ** (-0.5) * math.log2(math.e)


mark = jax.named_scope


def rem(a, b):
    return lax.rem(a, jnp.int32(b))


def div(a, b):
    return lax.div(a, jnp.int32(b))


def dot(a, b):
    return jnp.dot(a, b, preferred_element_type=F32)


def dot_t(a, b):
    return lax.dot_general(a, b, (((1,), (1,)), ((), ())), preferred_element_type=F32)


def kernel(
    window_ref,
    blocks_ref,
    tokens_hbm,
    gains_hbm,
    sq_hbm,
    skv_hbm,
    so_hbm,
    shkv_hbm,
    cq_hbm,
    co_hbm,
    out_ref,
    gains_ref,
    sq,
    skv,
    so,
    shkv,
    wall,
    xg,
    rs,
    ob,
    xs,
    acc,
    qs,
    ctx,
    own_kv,
    halo,
    kc,
    vc,
    sc,
    den,
    oacc,
    load_sem,
    own_sem,
    ag_send,
    ag_recv,
    rs_send,
    rs_recv,
    halo_send,
    halo_recv,
    wz_send,
    wz_recv,
    wx_send,
    wx_first,
    wx_recv,
    wy_send,
    wy_first,
    wy_recv,
    ws_send,
    ws_recv,
    cz_send,
    cz_recv,
    cx_send,
    cx_recv,
    cs_send,
    cs_recv,
):
    seq = lax.axis_index("seq")
    head = lax.axis_index("head")
    core = rem(seq, 2)
    xp = rem(div(seq, 2), 4)
    zh = div(seq, 8)
    yp = div(head, 2)
    zl = rem(head, 2)

    def seq_at(zz, xx, cc):
        return zz * 8 + xx * 2 + cc

    def head_to(k):
        return rem(yp + div(k, 2), 4) * 2 + rem(zl + rem(k, 2), 2)

    def head_from(k):
        return rem(yp + 4 - div(k, 2), 4) * 2 + rem(zl + rem(k, 2), 2)

    z_to = [rem(zh + d, 4) for d in (1, 2, 3)]
    z_from = [rem(zh + 4 - d, 4) for d in (1, 2, 3)]
    x_to = [rem(xp + d, 4) for d in (1, 2, 3)]
    x_from = [rem(xp + 4 - d, 4) for d in (1, 2, 3)]
    sibling = seq_at(zh, xp, 1 - core)
    following = rem(seq + 1, 32)
    previous = rem(seq + 31, 32)

    def rows_half(h):
        return pl.ds(h * HALF, HALF)

    barrier = pltpu.get_barrier_semaphore()

    def greet(s, h):
        pl.semaphore_signal(barrier, inc=1, device_id=(s, h), device_id_type=MESH)

    for zz in z_to:
        greet(seq_at(zz, xp, core), head)
    for k in range(1, 8):
        greet(seq, head_to(jnp.int32(k)))
    for xx in x_to:
        greet(seq_at(zh, xx, core), head)
    greet(sibling, head)
    greet(following, head)
    greet(previous, head)

    loads = [
        pltpu.make_async_copy(a, b, load_sem.at[i])
        for i, (a, b) in enumerate(
            (
                (tokens_hbm.at[rows_half(0)], xg.at[0, head]),
                (tokens_hbm.at[rows_half(1)], xg.at[1, head]),
                (gains_hbm, gains_ref),
                (skv_hbm, skv),
                (sq_hbm, sq),
                (so_hbm, so),
                (shkv_hbm, shkv),
            )
        )
    ]
    for copy in loads:
        copy.start()

    def piece_source(p):
        return (cq_hbm if p % 2 == 0 else co_hbm).at[p // 2]

    owns = [
        pltpu.make_async_copy(piece_source(p), wall.at[p, zh, xp, core], own_sem)
        for p in range(6)
    ]
    for copy in owns:
        copy.start()

    with mark("barrier"):
        pl.semaphore_wait(barrier, 16)

    def remote(src, dst, send, recv, s, h):
        return pltpu.make_async_remote_copy(
            src_ref=src, dst_ref=dst, send_sem=send, recv_sem=recv, device_id=(s, h), device_id_type=MESH
        )

    def take(ref, sem):
        pltpu.make_async_copy(ref, ref, sem).wait()

    beside_z = yp * 2 + 1 - zl

    def ag_slot(k):
        return 0 if k == 1 else 1 + k % 2

    def ag_out(h, k, src):
        return remote(
            src, xg.at[h, head], ag_send.at[h], ag_recv.at[h, ag_slot(k)], seq, head_to(jnp.int32(k))
        )

    def ag_pass(h, k):
        part = xg.at[h, beside_z]
        return remote(part, part, ag_send.at[h], ag_recv.at[h, ag_slot(k)], seq, head_to(jnp.int32(k - 1)))

    def ag_start(h, src):
        for k in (1, 2, 6, 4):
            ag_out(h, k, src).start()

    def ag_forward(h):
        with mark("forward"):
            take(xg.at[h, 0], ag_recv.at[h, 0])
            for k in (3, 7, 5):
                ag_pass(h, k).start()

    def ag_near(h):
        take(xg.at[h, pl.ds(0, 3)], ag_recv.at[h, 1])

    def ag_far(h):
        take(xg.at[h, pl.ds(0, 3)], ag_recv.at[h, 2])

    def ag_drain(h):
        take(xg.at[h, pl.ds(0, 7)], ag_send.at[h])

    def rs_copy(h, k):
        to = head_to(jnp.int32(k))
        return remote(ob.at[h, to], rs.at[h, k], rs_send.at[h], rs_recv.at[h], seq, to)

    beside_zh = (z_to[0], z_to[2])
    direct = (3,)

    def wz_copy(p, i, src, dst):
        to = beside_zh[i] if i < 2 else (z_to[1] if p in direct else beside_zh[i - 2])
        step = i // 2 if p not in direct else 0
        return remote(src, dst, wz_send, wz_recv.at[p, step], seq_at(to, xp, core), head)

    def wz_part(p, i, zz):
        if i < 2 or p in direct:
            return wall.at[p, zz, xp, core]
        return wall.at[p, zz, xp, core, pl.ds((i - 2) * (PIECE // 2), PIECE // 2)]

    def wz_out(p, i):
        if i < 2 or p in direct:
            return wz_copy(p, i, piece_source(p), wz_part(p, i, zh))
        part = wz_part(p, i, beside_zh[3 - i])
        return wz_copy(p, i, part, part)

    beside = (x_to[0], x_to[2])

    others = [rem(zh + d, 4) for d in (1, 2, 3)]

    def wx_out(p, zz, i, recv):
        src = piece_source(p) if zz is zh else wall.at[p, zz, xp, core]
        return remote(src, wall.at[p, zz, xp, core], wx_send, recv, seq_at(zh, beside[i], core), head)

    def wy_out(p, zz, i, recv):
        part = wall.at[p, zz, beside[1 - i], core, pl.ds(i * (PIECE // 2), PIECE // 2)]
        return remote(part, part, wy_send, recv, seq_at(zh, beside[i], core), head)

    def own_row_x():
        for p in range(6):
            for i in range(2):
                wx_out(p, zh, i, wx_first).start()

    def own_row_y():
        with mark("own_row_y"):
            take(wall.at[:, 0, 0], wx_first)
            for p in range(6):
                for i in range(2):
                    wy_out(p, zh, i, wy_first).start()

    def ws_out(p):
        part = wall.at[p, :, :, core]
        return remote(part, part, ws_send, ws_recv.at[p], sibling, head)

    def weight_z(p):
        for i in (0, 1, 2) if p in direct else (0, 1):
            wz_out(p, i).start()

    def weight_f(p):
        with mark("weight_f"):
            take(wall.at[p, 0, 0], wz_recv.at[p, 0])
            for i in (0, 1):
                wz_out(p, i + 2).start()

    def weight_x(p):
        with mark("weight_x"):
            if p in direct:
                take(wall.at[p, pl.ds(0, 3), 0, 0], wz_recv.at[p, 0])
            else:
                take(wall.at[p, 0, 0, 0], wz_recv.at[p, 1])
            for zz in others:
                for i in range(2):
                    wx_out(p, zz, i, wx_recv.at[p]).start()

    def weight_y(p):
        with mark("weight_y"):
            take(wall.at[p, pl.ds(0, 3), 0], wx_recv.at[p])
            for zz in others:
                for i in range(2):
                    wy_out(p, zz, i, wy_recv.at[p]).start()

    def weight_s(p):
        with mark("weight_s"):
            if p == 0:
                take(wall.at[:, 0, 0, 0], wy_first)
            take(wall.at[p, pl.ds(0, 3), 0, 0], wy_recv.at[p])
            ws_out(p).start()

    def weight_wait(p):
        with mark("weight_wait"):
            take(wall.at[p, :, :, 0], ws_recv.at[p])

    cache = (kc, vc)

    def cz_part(c, h, zz):
        return cache[c].at[zz, xp, core, rows_half(h)]

    def cz_out(c, h, i):
        part = cz_part(c, h, zh)
        return remote(part, part, cz_send, cz_recv.at[c, h, i], seq_at(z_to[i], xp, core), head)

    def cz_in(c, h, i):
        part = cz_part(c, h, z_from[i])
        return remote(part, part, cz_send, cz_recv.at[c, h, i], seq_at(z_to[i], xp, core), head)

    def cx_out(c, h, m, i):
        part = cz_part(c, h, rem(zh + 4 - m, 4))
        return remote(part, part, cx_send, cx_recv.at[c, h], seq_at(zh, x_to[i], core), head)

    def cs_out(c, h):
        part = cache[c].at[:, :, core, rows_half(h)]
        return remote(part, part, cs_send, cs_recv.at[c], sibling, head)

    def cols_of(j):
        return pl.ds(pl.multiple_of(j * COLS, 128), COLS)

    def gain(row, j):
        return gains_ref[row : row + 1, cols_of(j)]

    def square_sum(xf):
        sq2 = xf * xf
        return sq2[:, :HEAD] + sq2[:, HEAD : 2 * HEAD] + sq2[:, 2 * HEAD :]

    def row_factor(squares):
        return lax.rsqrt(jnp.sum(squares, axis=1, keepdims=True) / WIDTH + EPSILON)

    def plane(h, zz, row):
        parts, squares = [], 0.0
        for y in range(4):
            j = y * 2 + zz
            xf = xg[h, j].astype(F32)
            squares = squares + square_sum(xf)
            parts.append((xf * gain(row, j)).astype(BF16))
        return jnp.concatenate(parts, axis=1), squares

    def key_value_rows(ref, zz):
        keys = jnp.concatenate([ref[0, cols_of(y * 2 + zz)] for y in range(4)], axis=0)
        values = jnp.concatenate([ref[1, cols_of(y * 2 + zz)] for y in range(4)], axis=0)
        return jnp.concatenate([keys, values], axis=1)

    def piece_rows(p, zz):
        return wall[p, :, pl.ds(zz * 2, 2)].reshape(4 * COLS, COLS)

    def stack_query(h, full, factor):
        scaled = full * (factor * SCORE_SCALE)
        for g in range(GROUP):
            qs[h, g * HALF : (g + 1) * HALF, :] = scaled[:, g * HEAD : (g + 1) * HEAD].astype(BF16)

    def spread_context():
        inv = 1.0 / jnp.sum(den[...], axis=1, keepdims=True)
        c = (oacc[...] * inv).astype(BF16)
        for g in range(GROUP):
            ctx[:, g * HEAD : (g + 1) * HEAD] = c[g * HALF : (g + 1) * HALF, :]

    far = (3, 7, 5, 1)
    near = (4, 2, 6)

    def reduce_out(h, plane_of):
        with mark("rs_out"):
            for zz, ks in ((1 - zl, far), (zl, near)):
                for y, block in enumerate(plane_of(zz)):
                    ob[h, y * 2 + zz] = block.astype(BF16)
                for k in ks:
                    rs_copy(h, k).start()

    def reduce_in(h):
        with mark("rs_in"):
            take(rs.at[h, pl.ds(1, 7)], rs_recv.at[h])
            total = xs[h] + ob[h, head].astype(F32)
            for k in near + far:
                total = total + rs[h, k].astype(F32)
        return total

    def rs_drain(h):
        take(ob.at[h, pl.ds(0, 7)], rs_send.at[h])

    def own_part(h):
        return xg.at[h, head]

    for h in range(2):
        ag_start(h, tokens_hbm.at[rows_half(h)])
    weight_z(0)
    own_row_x()
    for h in range(2):
        ag_forward(h)
    weight_z(1)
    for copy in loads[:5]:
        copy.wait()

    def halo_of(h):
        return remote(
            own_kv.at[:, rows_half(h)], halo.at[:, rows_half(h)], halo_send, halo_recv, following, head
        )

    for h in range(2):
        xs[h] = xg[h, head].astype(F32)
        with mark("ag0"):
            ag_near(h)
            hb, squares = plane(h, zl, 0)
            acc[:, COLS:] = dot(hb, key_value_rows(skv, zl))
            acc[:, :COLS] = dot(hb, jnp.concatenate([sq[cols_of(y * 2 + zl)] for y in range(4)], axis=0))
            ag_far(h)
            hb, more = plane(h, 1 - zl, 0)
            factor = row_factor(squares + more)
            kv = (acc[:, COLS:] + dot(hb, key_value_rows(skv, 1 - zl))) * factor
            own_kv[0, rows_half(h)] = kv[:, :HEAD].astype(BF16)
            own_kv[1, rows_half(h)] = kv[:, HEAD:].astype(BF16)
            halo_of(h).start()
            full = acc[:, :COLS] + dot(
                hb, jnp.concatenate([sq[cols_of(y * 2 + 1 - zl)] for y in range(4)], axis=0)
            )
            stack_query(h, full, factor)
        weight_f(h)
    own_row_y()
    for h in range(2):
        ag_drain(h)

    col = lax.broadcasted_iota(jnp.int32, (1, 2 * ROWS), 1)
    loads[5].wait()
    with mark("halo"):
        take(halo, halo_recv)
    for h in range(2):
        row = lax.broadcasted_iota(jnp.int32, (HALF, 1), 0) + h * HALF
        offset = row + ROWS - col
        present = (offset >= 0) & (col >= jnp.where(seq == 0, ROWS, 0))
        with mark("self_attn"):
            for g in range(GROUP):
                here = slice(g * HALF, (g + 1) * HALF)
                qg = qs[h, here, :]
                score = jnp.concatenate([dot_t(qg, halo[0]), dot_t(qg, own_kv[0])], axis=1)
                score = jnp.where(present & (offset < window_ref[g]), score, MASKED)
                top = jnp.max(score, axis=1, keepdims=True)
                weights = jnp.exp2(score - top)
                den[here, :] = weights[:, :ROWS] + weights[:, ROWS:]
                wb = weights.astype(BF16)
                oacc[here, :] = dot(wb[:, :ROWS], halo[1]) + dot(wb[:, ROWS:], own_kv[1])
            spread_context()
        cvals = ctx[...]
        reduce_out(h, lambda zz, cvals=cvals: [dot(cvals, so[:, cols_of(y * 2 + zz)]) for y in range(4)])
        if h == 0:
            take(wall.at[:, 0, 0, 0], own_sem)
        weight_x(h)
    for h in range(2):
        total = reduce_in(h)
        xs[h] = total
        xg[h, head] = total.astype(BF16)
        ag_start(h, own_part(h))
        if h == 0:
            weight_z(2)
            ag_forward(0)
            weight_y(0)
        else:
            weight_z(4)
    loads[6].wait()

    factors = []
    for h in range(2):
        with mark("ag1"):
            ag_near(h)
            hb, squares = plane(h, zl, 1)
            acc[:, COLS:] = dot(hb, key_value_rows(shkv, zl))
            if h == 0:
                ag_forward(1)
            ag_far(h)
            hb, more = plane(h, 1 - zl, 1)
            factor = row_factor(squares + more)
            kv = (acc[:, COLS:] + dot(hb, key_value_rows(shkv, 1 - zl))) * factor
        factors.append(factor)
        for c in range(2):
            cache[c][zh, xp, core, rows_half(h)] = kv[:, c * HEAD : (c + 1) * HEAD].astype(BF16)
            for i in range(3):
                cz_out(c, h, i).start()
            for i in range(3):
                cx_out(c, h, 0, i).start()
        if h == 0:
            weight_y(1)
    weight_f(2)
    weight_f(4)
    weight_s(0)
    weight_z(3)
    weight_z(5)
    with mark("cache_z"):
        for h in range(2):
            for c in range(2):
                for m in (1, 2, 3):
                    cz_in(c, h, m - 1).wait_recv()
                    for i in range(3):
                        cx_out(c, h, m, i).start()
    weight_x(2)
    weight_s(1)
    weight_wait(0)
    for h in range(2):
        rs_drain(h)
        with mark("q0"):
            full = 0.0
            for zz in (0, 1):
                hb, _ = plane(h, zz, 2)
                full = full + dot(hb, piece_rows(0, zz))
        stack_query(h, full, factors[h])
        ag_drain(h)
    with mark("cache_x"):
        for h in range(2):
            for c in range(2):
                take(cache[c].at[:, pl.ds(0, 3), 0, rows_half(0)], cx_recv.at[c, h])
                cs_out(c, h).start()
    with mark("cache_s"):
        for c in range(2):
            take(cache[c].at[:, :, 0], cs_recv.at[c])

    half_row = rem(lax.broadcasted_iota(jnp.int32, (GROUP * HALF, 1), 0), HALF)
    causal_col = jnp.where(col < ROWS, col, -1)

    for section in range(3):
        for h in range(2):
            if section > 0:
                if h == 0:
                    weight_wait(2 * section)
                with mark("ag"):
                    ag_near(h)
                    hb, squares = plane(h, zl, 2 + section)
                    acc[:, :COLS] = dot(hb, piece_rows(2 * section, zl))
                    if h == 0:
                        if section == 1:
                            weight_x(5)
                        ag_forward(1)
                        weight_s(3 if section == 1 else 5)
                    ag_far(h)
                    hb, more = plane(h, 1 - zl, 2 + section)
                    full = acc[:, :COLS] + dot(hb, piece_rows(2 * section, 1 - zl))
                    stack_query(h, full, row_factor(squares + more))

            qv = qs[h]

            def pick(ref, i, section=section):
                n = jnp.maximum(blocks_ref[section, 0, i], 0)
                return ref[div(n, 8), rem(div(n, 2), 4), rem(n, 2)]

            with mark("score"):
                best = None
                for i in range(8):
                    keys = jnp.concatenate([pick(kc, 2 * i), pick(kc, 2 * i + 1)], axis=0)
                    t = dot_t(qv, keys)
                    low = jnp.where(blocks_ref[section, 0, 2 * i] >= 0, 0.0, MASKED)
                    high = jnp.where(blocks_ref[section, 0, 2 * i + 1] >= 0, 0.0, MASKED)
                    if i == 0:
                        t = jnp.where(causal_col <= half_row + h * HALF, t, MASKED)
                    t = t + jnp.where(col < ROWS, low, high)
                    sc[i] = t
                    pair = jnp.maximum(t[:, :HEAD], t[:, HEAD:])
                    best = pair if best is None else jnp.maximum(best, pair)
                top = jnp.max(best, axis=1, keepdims=True)
            if section > 0:
                ag_drain(h)

            with mark("value"):
                dens, outs = None, None
                for i in range(8):
                    weights = jnp.exp2(sc[i] - top)
                    part = weights[:, :HEAD] + weights[:, HEAD:]
                    dens = part if dens is None else dens + part
                    values = jnp.concatenate([pick(vc, 2 * i), pick(vc, 2 * i + 1)], axis=0)
                    part = dot(weights.astype(BF16), values)
                    outs = part if outs is None else outs + part
                den[...] = dens
                oacc[...] = outs
            spread_context()
            if h == 0:
                weight_wait(2 * section + 1)
            cvals = ctx[...]
            if section > 0:
                rs_drain(h)

            def plane_of(zz, cvals=cvals, section=section):
                wide = dot_t(cvals, piece_rows(2 * section + 1, zz))
                return [wide[:, y * COLS : (y + 1) * COLS] for y in range(4)]

            reduce_out(h, plane_of)
            if section == 0 and h == 0:
                weight_x(3)
            elif section == 0:
                weight_y(2)
            elif section == 1:
                weight_y(4 + h)
        for h in range(2):
            total = reduce_in(h)
            if section < 2:
                xs[h] = total
                xg[h, head] = total.astype(BF16)
                ag_start(h, own_part(h))
                if section == 0 and h == 0:
                    weight_f(5)
                    weight_y(3)
                    weight_x(4)
                    weight_s(2)
                elif section == 1 and h == 0:
                    weight_s(4)
                if h == 0:
                    ag_forward(0)
            else:
                out_ref[rows_half(h), :] = total
    with mark("tail"):
        for h in range(2):
            rs_drain(h)

    take(own_kv, halo_send)
    take(wall.at[pl.ds(0, 3), pl.ds(0, 3), 0], wz_send)
    take(wall.at[:, :, 0], wx_send)
    take(wall.at[:, pl.ds(0, 2), 0], wy_send)
    take(wall.at[:, :, :, 0], ws_send)
    take(kc.at[pl.ds(0, 3), 0], cz_send)
    take(kc.at[pl.ds(0, 3)], cx_send)
    take(kc, cs_send)


def body(
    tokens,
    norm_gains,
    window,
    self_query,
    self_key_value,
    self_output,
    shared_key_value,
    cross_query,
    cross_output,
    key_blocks,
):
    vmem = pl.BlockSpec(memory_space=pltpu.VMEM)
    smem = pl.BlockSpec(memory_space=pltpu.SMEM)
    hbm = pl.BlockSpec(memory_space=pl.ANY)
    dma = pltpu.SemaphoreType.DMA
    return pl.pallas_call(
        kernel,
        out_shape=jax.ShapeDtypeStruct((ROWS, COLS), F32),
        in_specs=[smem, smem] + [hbm] * 8,
        out_specs=vmem,
        scratch_shapes=[
            pltpu.VMEM((5, WIDTH), F32),
            pltpu.VMEM((WIDTH, COLS), BF16),
            pltpu.VMEM((2, WIDTH, HEAD), BF16),
            pltpu.VMEM((COLS, WIDTH), BF16),
            pltpu.VMEM((2, WIDTH, HEAD), BF16),
            pltpu.VMEM((6, 4, 4, 2, PIECE, COLS), BF16),
            pltpu.VMEM((2, 8, HALF, COLS), BF16),
            pltpu.VMEM((2, 8, HALF, COLS), BF16),
            pltpu.VMEM((2, 8, HALF, COLS), BF16),
            pltpu.VMEM((2, HALF, COLS), F32),
            pltpu.VMEM((HALF, COLS + 2 * HEAD), F32),
            pltpu.VMEM((2, GROUP * HALF, HEAD), BF16),
            pltpu.VMEM((HALF, COLS), BF16),
            pltpu.VMEM((2, ROWS, HEAD), BF16),
            pltpu.VMEM((2, ROWS, HEAD), BF16),
            pltpu.VMEM((4, 4, 2, ROWS, HEAD), BF16),
            pltpu.VMEM((4, 4, 2, ROWS, HEAD), BF16),
            pltpu.VMEM((8, GROUP * HALF, 2 * HEAD), F32),
            pltpu.VMEM((GROUP * HALF, HEAD), F32),
            pltpu.VMEM((GROUP * HALF, HEAD), F32),
            dma((7,)),
            dma,
            dma((2,)),
            dma((2, 3)),
            dma((2,)),
            dma((2,)),
            dma,
            dma,
            dma,
            dma((6, 2)),
            dma,
            dma,
            dma((6,)),
            dma,
            dma,
            dma((6,)),
            dma,
            dma((6,)),
            dma,
            dma((2, 2, 3)),
            dma,
            dma((2, 2)),
            dma,
            dma((2,)),
        ],
        compiler_params=pltpu.CompilerParams(
            collective_id=0, has_side_effects=True, vmem_limit_bytes=60 * 1024 * 1024
        ),
        name="window",
    )(
        window,
        key_blocks,
        tokens,
        norm_gains,
        self_query,
        self_key_value,
        self_output,
        shared_key_value,
        cross_query,
        jnp.swapaxes(cross_output, 1, 2),
    )


def solution(mesh):
    placed = (
        P("seq", "head"),
        P(),
        P("head"),
        P(None, "head"),
        P(None, None, "head"),
        P("head", None),
        P(None, None, "head"),
        P(None, "seq", "head"),
        P(None, "head", "seq"),
        P(None, "seq", None),
    )
    return jax.shard_map(
        body, mesh=mesh, in_specs=placed, out_specs=P("seq", "head"), check_vma=False
    )
```

```python
import math

import jax
import jax.numpy as jnp
from jax import lax
from jax.experimental import pallas as pl
from jax.experimental.pallas import tpu as pltpu
from jax.sharding import PartitionSpec as P

MESH = pl.DeviceIdType.MESH
EPSILON = 1e-06
MASKED = -1e30
F32 = jnp.float32
BF16 = jnp.bfloat16
WIDTH = 3072
ROWS = 128
COLS = 384
HEAD = 128
GROUP = 3
PIECE = 96
HALF = 64
SCORE_SCALE = HEAD ** (-0.5) * math.log2(math.e)


mark = jax.named_scope


def rem(a, b):
    return lax.rem(a, jnp.int32(b))


def div(a, b):
    return lax.div(a, jnp.int32(b))


def dot(a, b):
    return jnp.dot(a, b, preferred_element_type=F32)


def dot_t(a, b):
    return lax.dot_general(a, b, (((1,), (1,)), ((), ())), preferred_element_type=F32)


def kernel(
    window_ref,
    blocks_ref,
    tokens_hbm,
    gains_hbm,
    sq_hbm,
    skv_hbm,
    so_hbm,
    shkv_hbm,
    cq_hbm,
    co_hbm,
    out_ref,
    gains_ref,
    sq,
    skv,
    so,
    shkv,
    wall,
    xg,
    rs,
    ob,
    xs,
    acc,
    qs,
    ctx,
    own_kv,
    halo,
    kc,
    vc,
    sc,
    den,
    oacc,
    load_sem,
    own_sem,
    ag_send,
    ag_recv,
    rs_send,
    rs_recv,
    halo_send,
    halo_recv,
    wz_send,
    wz_recv,
    wx_send,
    wx_first,
    wx_recv,
    wy_send,
    wy_first,
    wy_recv,
    ws_send,
    ws_recv,
    cz_send,
    cz_recv,
    cx_send,
    cx_recv,
    cs_send,
    cs_recv,
):
    seq = lax.axis_index("seq")
    head = lax.axis_index("head")
    core = rem(seq, 2)
    xp = rem(div(seq, 2), 4)
    zh = div(seq, 8)
    yp = div(head, 2)
    zl = rem(head, 2)

    def seq_at(zz, xx, cc):
        return zz * 8 + xx * 2 + cc

    def head_to(k):
        return rem(yp + div(k, 2), 4) * 2 + rem(zl + rem(k, 2), 2)

    def head_from(k):
        return rem(yp + 4 - div(k, 2), 4) * 2 + rem(zl + rem(k, 2), 2)

    z_to = [rem(zh + d, 4) for d in (1, 2, 3)]
    z_from = [rem(zh + 4 - d, 4) for d in (1, 2, 3)]
    x_to = [rem(xp + d, 4) for d in (1, 2, 3)]
    x_from = [rem(xp + 4 - d, 4) for d in (1, 2, 3)]
    sibling = seq_at(zh, xp, 1 - core)
    following = rem(seq + 1, 32)
    previous = rem(seq + 31, 32)

    def rows_half(h):
        return pl.ds(h * HALF, HALF)

    barrier = pltpu.get_barrier_semaphore()

    def greet(s, h):
        pl.semaphore_signal(barrier, inc=1, device_id=(s, h), device_id_type=MESH)

    for zz in z_to:
        greet(seq_at(zz, xp, core), head)
    for k in range(1, 8):
        greet(seq, head_to(jnp.int32(k)))
    for xx in x_to:
        greet(seq_at(zh, xx, core), head)
    greet(sibling, head)
    greet(following, head)
    greet(previous, head)

    loads = [
        pltpu.make_async_copy(a, b, load_sem.at[i])
        for i, (a, b) in enumerate(
            (
                (tokens_hbm.at[rows_half(0)], xg.at[0, head]),
                (tokens_hbm.at[rows_half(1)], xg.at[1, head]),
                (gains_hbm, gains_ref),
                (skv_hbm, skv),
                (sq_hbm, sq),
                (so_hbm, so),
                (shkv_hbm, shkv),
            )
        )
    ]
    for copy in loads:
        copy.start()

    def piece_source(p):
        return (cq_hbm if p % 2 == 0 else co_hbm).at[p // 2]

    owns = [
        pltpu.make_async_copy(piece_source(p), wall.at[p, zh, xp, core], own_sem)
        for p in range(6)
    ]
    for copy in owns:
        copy.start()

    with mark("barrier"):
        pl.semaphore_wait(barrier, 16)

    def remote(src, dst, send, recv, s, h):
        return pltpu.make_async_remote_copy(
            src_ref=src, dst_ref=dst, send_sem=send, recv_sem=recv, device_id=(s, h), device_id_type=MESH
        )

    def take(ref, sem):
        pltpu.make_async_copy(ref, ref, sem).wait()

    beside_z = yp * 2 + 1 - zl

    def ag_slot(k):
        return 0 if k == 1 else 1 + k % 2

    def ag_out(h, k, src):
        return remote(
            src, xg.at[h, head], ag_send.at[h], ag_recv.at[h, ag_slot(k)], seq, head_to(jnp.int32(k))
        )

    def ag_pass(h, k):
        part = xg.at[h, beside_z]
        return remote(part, part, ag_send.at[h], ag_recv.at[h, ag_slot(k)], seq, head_to(jnp.int32(k - 1)))

    def ag_start(h, src):
        for k in (1, 2, 6, 4):
            ag_out(h, k, src).start()

    def ag_forward(h):
        with mark("forward"):
            take(xg.at[h, 0], ag_recv.at[h, 0])
            for k in (3, 7, 5):
                ag_pass(h, k).start()

    def ag_near(h):
        take(xg.at[h, pl.ds(0, 3)], ag_recv.at[h, 1])

    def ag_far(h):
        take(xg.at[h, pl.ds(0, 3)], ag_recv.at[h, 2])

    def ag_drain(h):
        take(xg.at[h, pl.ds(0, 7)], ag_send.at[h])

    def rs_copy(h, k):
        to = head_to(jnp.int32(k))
        return remote(ob.at[h, to], rs.at[h, k], rs_send.at[h], rs_recv.at[h], seq, to)

    beside_zh = (z_to[0], z_to[2])
    direct = (3,)

    def wz_copy(p, i, src, dst):
        to = beside_zh[i] if i < 2 else (z_to[1] if p in direct else beside_zh[i - 2])
        step = i // 2 if p not in direct else 0
        return remote(src, dst, wz_send, wz_recv.at[p, step], seq_at(to, xp, core), head)

    def wz_part(p, i, zz):
        if i < 2 or p in direct:
            return wall.at[p, zz, xp, core]
        return wall.at[p, zz, xp, core, pl.ds((i - 2) * (PIECE // 2), PIECE // 2)]

    def wz_out(p, i):
        if i < 2 or p in direct:
            return wz_copy(p, i, piece_source(p), wz_part(p, i, zh))
        part = wz_part(p, i, beside_zh[3 - i])
        return wz_copy(p, i, part, part)

    beside = (x_to[0], x_to[2])

    others = [rem(zh + d, 4) for d in (1, 2, 3)]

    def wx_out(p, zz, i, recv):
        src = piece_source(p) if zz is zh else wall.at[p, zz, xp, core]
        return remote(src, wall.at[p, zz, xp, core], wx_send, recv, seq_at(zh, beside[i], core), head)

    def wy_out(p, zz, i, recv):
        part = wall.at[p, zz, beside[1 - i], core, pl.ds(i * (PIECE // 2), PIECE // 2)]
        return remote(part, part, wy_send, recv, seq_at(zh, beside[i], core), head)

    def own_row_x():
        for p in range(6):
            for i in range(2):
                wx_out(p, zh, i, wx_first).start()

    def own_row_y():
        with mark("own_row_y"):
            take(wall.at[:, 0, 0], wx_first)
            for p in range(6):
                for i in range(2):
                    wy_out(p, zh, i, wy_first).start()

    def ws_out(p):
        part = wall.at[p, :, :, core]
        return remote(part, part, ws_send, ws_recv.at[p], sibling, head)

    def weight_z(p):
        for i in (0, 1, 2) if p in direct else (0, 1):
            wz_out(p, i).start()

    def weight_f(p):
        with mark("weight_f"):
            take(wall.at[p, 0, 0], wz_recv.at[p, 0])
            for i in (0, 1):
                wz_out(p, i + 2).start()

    def weight_x(p):
        with mark("weight_x"):
            if p in direct:
                take(wall.at[p, pl.ds(0, 3), 0, 0], wz_recv.at[p, 0])
            else:
                take(wall.at[p, 0, 0, 0], wz_recv.at[p, 1])
            for zz in others:
                for i in range(2):
                    wx_out(p, zz, i, wx_recv.at[p]).start()

    def weight_y(p):
        with mark("weight_y"):
            take(wall.at[p, pl.ds(0, 3), 0], wx_recv.at[p])
            for zz in others:
                for i in range(2):
                    wy_out(p, zz, i, wy_recv.at[p]).start()

    def weight_s(p):
        with mark("weight_s"):
            if p == 0:
                take(wall.at[:, 0, 0, 0], wy_first)
            take(wall.at[p, pl.ds(0, 3), 0, 0], wy_recv.at[p])
            ws_out(p).start()

    def weight_wait(p):
        with mark("weight_wait"):
            take(wall.at[p, :, :, 0], ws_recv.at[p])

    cache = (kc, vc)

    def cz_part(c, h, zz):
        return cache[c].at[zz, xp, core, rows_half(h)]

    def cz_out(c, h, i):
        part = cz_part(c, h, zh)
        return remote(part, part, cz_send, cz_recv.at[c, h, i], seq_at(z_to[i], xp, core), head)

    def cz_in(c, h, i):
        part = cz_part(c, h, z_from[i])
        return remote(part, part, cz_send, cz_recv.at[c, h, i], seq_at(z_to[i], xp, core), head)

    def cx_out(c, h, m, i):
        part = cz_part(c, h, rem(zh + 4 - m, 4))
        return remote(part, part, cx_send, cx_recv.at[c, h], seq_at(zh, x_to[i], core), head)

    def cs_out(c, h):
        part = cache[c].at[:, :, core, rows_half(h)]
        return remote(part, part, cs_send, cs_recv.at[c], sibling, head)

    def cols_of(j):
        return pl.ds(pl.multiple_of(j * COLS, 128), COLS)

    def gain(row, j):
        return gains_ref[row : row + 1, cols_of(j)]

    def square_sum(xf):
        sq2 = xf * xf
        return sq2[:, :HEAD] + sq2[:, HEAD : 2 * HEAD] + sq2[:, 2 * HEAD :]

    def row_factor(squares):
        return lax.rsqrt(jnp.sum(squares, axis=1, keepdims=True) / WIDTH + EPSILON)

    def plane(h, zz, row):
        parts, squares = [], 0.0
        for y in range(4):
            j = y * 2 + zz
            xf = xg[h, j].astype(F32)
            squares = squares + square_sum(xf)
            parts.append((xf * gain(row, j)).astype(BF16))
        return jnp.concatenate(parts, axis=1), squares

    def key_value_rows(ref, zz):
        keys = jnp.concatenate([ref[0, cols_of(y * 2 + zz)] for y in range(4)], axis=0)
        values = jnp.concatenate([ref[1, cols_of(y * 2 + zz)] for y in range(4)], axis=0)
        return jnp.concatenate([keys, values], axis=1)

    def piece_rows(p, zz):
        return wall[p, :, pl.ds(zz * 2, 2)].reshape(4 * COLS, COLS)

    def stack_query(h, full, factor):
        scaled = full * (factor * SCORE_SCALE)
        for g in range(GROUP):
            qs[h, g * HALF : (g + 1) * HALF, :] = scaled[:, g * HEAD : (g + 1) * HEAD].astype(BF16)

    def spread_context():
        inv = 1.0 / jnp.sum(den[...], axis=1, keepdims=True)
        c = (oacc[...] * inv).astype(BF16)
        for g in range(GROUP):
            ctx[:, g * HEAD : (g + 1) * HEAD] = c[g * HALF : (g + 1) * HALF, :]

    far = (3, 7, 5, 1)
    near = (4, 2, 6)

    def reduce_out(h, plane_of):
        with mark("rs_out"):
            for zz, ks in ((1 - zl, far), (zl, near)):
                for y, block in enumerate(plane_of(zz)):
                    ob[h, y * 2 + zz] = block.astype(BF16)
                for k in ks:
                    rs_copy(h, k).start()

    def reduce_in(h):
        with mark("rs_in"):
            take(rs.at[h, pl.ds(1, 7)], rs_recv.at[h])
            total = xs[h] + ob[h, head].astype(F32)
            for k in near + far:
                total = total + rs[h, k].astype(F32)
        return total

    def rs_drain(h):
        take(ob.at[h, pl.ds(0, 7)], rs_send.at[h])

    def own_part(h):
        return xg.at[h, head]

    for h in range(2):
        ag_start(h, tokens_hbm.at[rows_half(h)])
    weight_z(0)
    own_row_x()
    for h in range(2):
        ag_forward(h)
    weight_z(1)
    for copy in loads[:5]:
        copy.wait()

    def halo_of(h):
        return remote(
            own_kv.at[:, rows_half(h)], halo.at[:, rows_half(h)], halo_send, halo_recv, following, head
        )

    for h in range(2):
        xs[h] = xg[h, head].astype(F32)
        with mark("ag0"):
            ag_near(h)
            hb, squares = plane(h, zl, 0)
            acc[:, COLS:] = dot(hb, key_value_rows(skv, zl))
            acc[:, :COLS] = dot(hb, jnp.concatenate([sq[cols_of(y * 2 + zl)] for y in range(4)], axis=0))
            ag_far(h)
            hb, more = plane(h, 1 - zl, 0)
            factor = row_factor(squares + more)
            kv = (acc[:, COLS:] + dot(hb, key_value_rows(skv, 1 - zl))) * factor
            own_kv[0, rows_half(h)] = kv[:, :HEAD].astype(BF16)
            own_kv[1, rows_half(h)] = kv[:, HEAD:].astype(BF16)
            halo_of(h).start()
            full = acc[:, :COLS] + dot(
                hb, jnp.concatenate([sq[cols_of(y * 2 + 1 - zl)] for y in range(4)], axis=0)
            )
            stack_query(h, full, factor)
        weight_f(h)
    own_row_y()
    for h in range(2):
        ag_drain(h)

    col = lax.broadcasted_iota(jnp.int32, (1, 2 * ROWS), 1)
    loads[5].wait()
    with mark("halo"):
        take(halo, halo_recv)
    for h in range(2):
        row = lax.broadcasted_iota(jnp.int32, (HALF, 1), 0) + h * HALF
        offset = row + ROWS - col
        present = (offset >= 0) & (col >= jnp.where(seq == 0, ROWS, 0))
        with mark("self_attn"):
            for g in range(GROUP):
                here = slice(g * HALF, (g + 1) * HALF)
                qg = qs[h, here, :]
                score = jnp.concatenate([dot_t(qg, halo[0]), dot_t(qg, own_kv[0])], axis=1)
                score = jnp.where(present & (offset < window_ref[g]), score, MASKED)
                top = jnp.max(score, axis=1, keepdims=True)
                weights = jnp.exp2(score - top)
                den[here, :] = weights[:, :ROWS] + weights[:, ROWS:]
                wb = weights.astype(BF16)
                oacc[here, :] = dot(wb[:, :ROWS], halo[1]) + dot(wb[:, ROWS:], own_kv[1])
            spread_context()
        cvals = ctx[...]
        reduce_out(h, lambda zz, cvals=cvals: [dot(cvals, so[:, cols_of(y * 2 + zz)]) for y in range(4)])
        if h == 0:
            take(wall.at[:, 0, 0, 0], own_sem)
        weight_x(h)
    for h in range(2):
        total = reduce_in(h)
        xs[h] = total
        xg[h, head] = total.astype(BF16)
        ag_start(h, own_part(h))
        if h == 0:
            weight_z(2)
            ag_forward(0)
            weight_y(0)
        else:
            weight_z(4)
    loads[6].wait()

    factors = []
    for h in range(2):
        with mark("ag1"):
            ag_near(h)
            hb, squares = plane(h, zl, 1)
            acc[:, COLS:] = dot(hb, key_value_rows(shkv, zl))
            if h == 0:
                ag_forward(1)
            ag_far(h)
            hb, more = plane(h, 1 - zl, 1)
            factor = row_factor(squares + more)
            kv = (acc[:, COLS:] + dot(hb, key_value_rows(shkv, 1 - zl))) * factor
        factors.append(factor)
        for c in range(2):
            cache[c][zh, xp, core, rows_half(h)] = kv[:, c * HEAD : (c + 1) * HEAD].astype(BF16)
            for i in range(3):
                cz_out(c, h, i).start()
            for i in range(3):
                cx_out(c, h, 0, i).start()
        if h == 0:
            weight_y(1)
    weight_f(2)
    weight_f(4)
    weight_s(0)
    weight_z(3)
    weight_z(5)
    with mark("cache_z"):
        for h in range(2):
            for c in range(2):
                for m in (1, 2, 3):
                    cz_in(c, h, m - 1).wait_recv()
                    for i in range(3):
                        cx_out(c, h, m, i).start()
    weight_x(2)
    weight_s(1)
    weight_wait(0)
    for h in range(2):
        rs_drain(h)
        with mark("q0"):
            full = 0.0
            for zz in (0, 1):
                hb, _ = plane(h, zz, 2)
                full = full + dot(hb, piece_rows(0, zz))
        stack_query(h, full, factors[h])
        ag_drain(h)
    with mark("cache_x"):
        for h in range(2):
            for c in range(2):
                take(cache[c].at[:, pl.ds(0, 3), 0, rows_half(0)], cx_recv.at[c, h])
                cs_out(c, h).start()
    with mark("cache_s"):
        take(kc.at[:, :, 0], cs_recv.at[0])

    half_row = rem(lax.broadcasted_iota(jnp.int32, (GROUP * HALF, 1), 0), HALF)
    causal_col = jnp.where(col < ROWS, col, -1)

    for section in range(3):
        for h in range(2):
            if section > 0:
                if h == 0:
                    weight_wait(2 * section)
                with mark("ag"):
                    ag_near(h)
                    hb, squares = plane(h, zl, 2 + section)
                    acc[:, :COLS] = dot(hb, piece_rows(2 * section, zl))
                    if h == 0:
                        if section == 1:
                            weight_x(5)
                        ag_forward(1)
                        weight_s(3 if section == 1 else 5)
                    ag_far(h)
                    hb, more = plane(h, 1 - zl, 2 + section)
                    full = acc[:, :COLS] + dot(hb, piece_rows(2 * section, 1 - zl))
                    stack_query(h, full, row_factor(squares + more))

            qv = qs[h]

            def pick(ref, i, section=section):
                n = jnp.maximum(blocks_ref[section, 0, i], 0)
                return ref[div(n, 8), rem(div(n, 2), 4), rem(n, 2)]

            with mark("score"):
                best = None
                for i in range(8):
                    keys = jnp.concatenate([pick(kc, 2 * i), pick(kc, 2 * i + 1)], axis=0)
                    t = dot_t(qv, keys)
                    low = jnp.where(blocks_ref[section, 0, 2 * i] >= 0, 0.0, MASKED)
                    high = jnp.where(blocks_ref[section, 0, 2 * i + 1] >= 0, 0.0, MASKED)
                    if i == 0:
                        t = jnp.where(causal_col <= half_row + h * HALF, t, MASKED)
                    t = t + jnp.where(col < ROWS, low, high)
                    sc[i] = t
                    pair = jnp.maximum(t[:, :HEAD], t[:, HEAD:])
                    best = pair if best is None else jnp.maximum(best, pair)
                top = jnp.max(best, axis=1, keepdims=True)
            if section > 0:
                ag_drain(h)

            if section == 0 and h == 0:
                with mark("cache_v"):
                    take(vc.at[:, :, 0], cs_recv.at[1])
            with mark("value"):
                dens, outs = None, None
                for i in range(8):
                    weights = jnp.exp2(sc[i] - top)
                    part = weights[:, :HEAD] + weights[:, HEAD:]
                    dens = part if dens is None else dens + part
                    values = jnp.concatenate([pick(vc, 2 * i), pick(vc, 2 * i + 1)], axis=0)
                    part = dot(weights.astype(BF16), values)
                    outs = part if outs is None else outs + part
                den[...] = dens
                oacc[...] = outs
            spread_context()
            if h == 0:
                weight_wait(2 * section + 1)
            cvals = ctx[...]
            if section > 0:
                rs_drain(h)

            def plane_of(zz, cvals=cvals, section=section):
                wide = dot_t(cvals, piece_rows(2 * section + 1, zz))
                return [wide[:, y * COLS : (y + 1) * COLS] for y in range(4)]

            reduce_out(h, plane_of)
            if section == 0 and h == 0:
                weight_x(3)
            elif section == 0:
                weight_y(2)
            elif section == 1:
                weight_y(4 + h)
        for h in range(2):
            total = reduce_in(h)
            if section < 2:
                xs[h] = total
                xg[h, head] = total.astype(BF16)
                ag_start(h, own_part(h))
                if section == 0 and h == 0:
                    weight_f(5)
                    weight_y(3)
                    weight_x(4)
                    weight_s(2)
                elif section == 1 and h == 0:
                    weight_s(4)
                if h == 0:
                    ag_forward(0)
            else:
                out_ref[rows_half(h), :] = total
    with mark("tail"):
        for h in range(2):
            rs_drain(h)

    take(own_kv, halo_send)
    take(wall.at[pl.ds(0, 3), pl.ds(0, 3), 0], wz_send)
    take(wall.at[:, :, 0], wx_send)
    take(wall.at[:, pl.ds(0, 2), 0], wy_send)
    take(wall.at[:, :, :, 0], ws_send)
    take(kc.at[pl.ds(0, 3), 0], cz_send)
    take(kc.at[pl.ds(0, 3)], cx_send)
    take(kc, cs_send)


def body(
    tokens,
    norm_gains,
    window,
    self_query,
    self_key_value,
    self_output,
    shared_key_value,
    cross_query,
    cross_output,
    key_blocks,
):
    vmem = pl.BlockSpec(memory_space=pltpu.VMEM)
    smem = pl.BlockSpec(memory_space=pltpu.SMEM)
    hbm = pl.BlockSpec(memory_space=pl.ANY)
    dma = pltpu.SemaphoreType.DMA
    return pl.pallas_call(
        kernel,
        out_shape=jax.ShapeDtypeStruct((ROWS, COLS), F32),
        in_specs=[smem, smem] + [hbm] * 8,
        out_specs=vmem,
        scratch_shapes=[
            pltpu.VMEM((5, WIDTH), F32),
            pltpu.VMEM((WIDTH, COLS), BF16),
            pltpu.VMEM((2, WIDTH, HEAD), BF16),
            pltpu.VMEM((COLS, WIDTH), BF16),
            pltpu.VMEM((2, WIDTH, HEAD), BF16),
            pltpu.VMEM((6, 4, 4, 2, PIECE, COLS), BF16),
            pltpu.VMEM((2, 8, HALF, COLS), BF16),
            pltpu.VMEM((2, 8, HALF, COLS), BF16),
            pltpu.VMEM((2, 8, HALF, COLS), BF16),
            pltpu.VMEM((2, HALF, COLS), F32),
            pltpu.VMEM((HALF, COLS + 2 * HEAD), F32),
            pltpu.VMEM((2, GROUP * HALF, HEAD), BF16),
            pltpu.VMEM((HALF, COLS), BF16),
            pltpu.VMEM((2, ROWS, HEAD), BF16),
            pltpu.VMEM((2, ROWS, HEAD), BF16),
            pltpu.VMEM((4, 4, 2, ROWS, HEAD), BF16),
            pltpu.VMEM((4, 4, 2, ROWS, HEAD), BF16),
            pltpu.VMEM((8, GROUP * HALF, 2 * HEAD), F32),
            pltpu.VMEM((GROUP * HALF, HEAD), F32),
            pltpu.VMEM((GROUP * HALF, HEAD), F32),
            dma((7,)),
            dma,
            dma((2,)),
            dma((2, 3)),
            dma((2,)),
            dma((2,)),
            dma,
            dma,
            dma,
            dma((6, 2)),
            dma,
            dma,
            dma((6,)),
            dma,
            dma,
            dma((6,)),
            dma,
            dma((6,)),
            dma,
            dma((2, 2, 3)),
            dma,
            dma((2, 2)),
            dma,
            dma((2,)),
        ],
        compiler_params=pltpu.CompilerParams(
            collective_id=0, has_side_effects=True, vmem_limit_bytes=60 * 1024 * 1024
        ),
        name="window",
    )(
        window,
        key_blocks,
        tokens,
        norm_gains,
        self_query,
        self_key_value,
        self_output,
        shared_key_value,
        cross_query,
        jnp.swapaxes(cross_output, 1, 2),
    )


def solution(mesh):
    placed = (
        P("seq", "head"),
        P(),
        P("head"),
        P(None, "head"),
        P(None, None, "head"),
        P("head", None),
        P(None, None, "head"),
        P(None, "seq", "head"),
        P(None, "head", "seq"),
        P(None, "seq", None),
    )
    return jax.shard_map(
        body, mesh=mesh, in_specs=placed, out_specs=P("seq", "head"), check_vma=False
    )
```
